32 devices in a mesh: seg: 8 (over z, x), lag: 4 (over y, core).
Axes of the slice: x: 2, y: 2, z: 4, core: 2. Of those that a mesh axis runs over, the one named last changes fastest.
Arguments:
- actuator_input: bfloat16 [24576, 256], P('seg'), may hold values from -6 to 6
- sensor_output: bfloat16 [24576, 2048], P('seg', 'lag'), may hold values from -6 to 6
- run_lengths: int32 [4], replicated, may hold values from 1 to 12288, 24576 in all
- lag_offsets: int32 [2], replicated, may hold values from 0 to 1022, as said below
Outputs:
- markov: float32 [256, 4, 2048], P('seg', 'lag')
The draws below stay inside these ranges and needn't reach their ends.
Inputs may be any that keep to these rules, and one draw needn't show every extreme that they name: `run_lengths`: the 4 lengths add up to 24576; at least one equals 12288. `lag_offsets`: at least one block starts at 1022.
All inputs are finite; a program needn't handle non-finite values.
Results may differ from the reference program's by a relative error of at most 0.0003.
Values may be sent and summed in bfloat16 or wider, within the bound.
No kernel may reach another device: no remote copies, remote signals or barrier semaphores. Data moves between devices by JAX's collectives and lax.ppermute only.
A program may use at most 64 MiB of HBM per device.

```python
import math
import jax
import jax.numpy as jnp
import numpy as np
from jax import lax

M = 256
P_SIZE = 2048
TD = 3072
LMAX = 1024
LBW = 2
NBLK = 2
NS = 24576
NSEG = 4
SEG_MOST = 12288


def draw_lag_offsets(key, part):
    first_key, second_key = jax.random.split(jax.random.fold_in(key, 11))
    values = jax.random.randint(first_key, (NBLK,), 0, LMAX - LBW, dtype=jnp.int32)
    place = jax.random.randint(second_key, (), 0, NBLK, dtype=jnp.int32)
    return jnp.where(jnp.arange(NBLK, dtype=jnp.int32) == place, LMAX - LBW, values).astype(jnp.int32)


def with_spikes(array, own_key, source, target, shards_of, factor):
    def block_of(position):
        return (jnp.arange(array.shape[position]) // (array.shape[position] // shards_of)).reshape((-1,) + (1,) * (array.ndim - 1 - position))

    one_side = jax.random.permutation(own_key, shards_of)[block_of(target)]
    other_side = (block_of(target) + shards_of // 2) % shards_of
    return jnp.where((block_of(source) == one_side) | (block_of(source) == other_side), factor * array, array)


def level_of(own_key, dims, cuts, low, largest):
    gain, own = 1.0, jax.random.fold_in(own_key, 6)
    for axis_at, parts in cuts:
        draws = jnp.exp(jax.random.uniform(jax.random.fold_in(own, axis_at), (parts,), jnp.float32, low / len(cuts), largest / len(cuts)))
        gain = gain * jnp.repeat(draws, dims[axis_at] // parts).reshape([-1 if axis == axis_at else 1 for axis in range(len(dims))])
    return gain


def length_profile(number_of, total, reach, lean):
    loads = [(1 << 20) // math.isqrt(standing ** lean) + 1 for standing in range(2, number_of + 1)]
    spare, holding = total - reach - (number_of - 1), [1] * (number_of - 1)
    while spare > 0:
        movable = [i for i in range(number_of - 1) if holding[i] < reach]
        whole, budget = sum([loads[i] for i in movable]), spare
        for i in movable:
            more = min(reach - holding[i], max(1, budget * loads[i] // whole), spare)
            holding[i] = holding[i] + more
            spare = spare - more
    return np.array([reach] + holding)


def uneven_parts(stream_key, number_of, total, reach, lean):
    if number_of == 2:
        one = jax.random.randint(stream_key, (), max(1, total - reach), min(reach, total - 1) + 1)
        return jnp.stack([one, total - one])
    tallies = jnp.asarray(length_profile(number_of, total, reach, lean), jnp.int32)
    couples = (number_of - 1) // 2
    giver, taker = tallies[1:1 + 2 * couples:2], tallies[2:2 + 2 * couples:2]
    margin = jnp.minimum(giver - 1, reach - taker)
    passed = jax.random.randint(jax.random.fold_in(stream_key, 1), (couples,), 0, 1 << 20) % (margin + 1)
    tallies = tallies.at[1:1 + 2 * couples:2].set(giver - passed).at[2:2 + 2 * couples:2].set(taker + passed)
    return tallies[jax.random.permutation(jax.random.fold_in(stream_key, 2), number_of)]


def normal_values(stream_key, dims, scale, reach, cuts=(), kind=jnp.bfloat16):
    values = jax.random.normal(stream_key, dims, jnp.float32) * scale
    if len(cuts) > 0:
        values = level_of(stream_key, dims, cuts, -0.22, 0.18) * values
    return jnp.clip(values, min=-reach, max=reach).astype(kind)


def noise_with(own_key, dims, scale, bound, cuts, heavy, held_as=jnp.bfloat16):
    array = scale * jax.random.normal(own_key, dims, jnp.float32)
    if cuts:
        array = array * level_of(own_key, dims, cuts, -0.22, 0.18)
    return jnp.clip(with_spikes(array, jax.random.fold_in(own_key, 3), *heavy), -bound, bound).astype(held_as)


def setup_inputs(seed: int = 0) -> dict:
    splits = jax.random.split(jax.random.key(seed), 5)
    return {
        "actuator_input": noise_with(splits[0], (NS, M), 1.0, 6.0, ((0, 8),), (0, 1, 8, 2.0)),
        "sensor_output": normal_values(splits[1], (NS, P_SIZE), 1.0, 6.0, ((0, 8), (1, 4))),
        "run_lengths": uneven_parts(splits[2], NSEG, NS, SEG_MOST, 2).astype(jnp.int32),
        "lag_offsets": draw_lag_offsets(jax.random.fold_in(splits[4], 71), 0),
    }


def segment_ids(run_lengths, start_row, row_count):
    run_ends = jnp.cumsum(run_lengths).astype(jnp.int32)
    places = (start_row + jnp.arange(row_count, dtype=jnp.int32)).astype(jnp.int32)
    return lax.optimization_barrier(jnp.sum((run_ends[None, :] <= places[:, None]).astype(jnp.int32), axis=1)).astype(jnp.int32)

def lag_table(lag_offsets):
    offsets_in = jnp.arange(LBW, dtype=jnp.int32)
    return (lag_offsets[:, None] + offsets_in[None, :]).reshape(-1).astype(jnp.int32)

def reference(actuator_input, sensor_output, run_lengths, lag_offsets):
    sample_count = actuator_input.shape[0]
    blocks = sample_count // TD
    idents = segment_ids(run_lengths, 0, sample_count + LMAX)
    shifts = lag_table(lag_offsets)
    actuator_blocks = actuator_input.reshape(blocks, TD, M)
    sensor_blocks = sensor_output.reshape(blocks, TD, P_SIZE)
    next_heads = jnp.concatenate([sensor_blocks[1:, :LMAX], jnp.zeros((1, LMAX, P_SIZE), sensor_output.dtype)], axis=0)

    def add_block(running, inputs):
        actuators, sensors, heads, blk_num = inputs
        joined = jnp.concatenate([sensors, heads], axis=0)
        window_ids = lax.dynamic_slice_in_dim(idents, (blk_num * TD).astype(jnp.int32), TD + LMAX, 0)
        own_ids = window_ids[:TD]

        def lag_product(lag_value):
            shifted = lax.dynamic_slice_in_dim(joined, lag_value, TD, 0)
            shifted_ids = lax.dynamic_slice_in_dim(window_ids, lag_value, TD, 0)
            masked = jnp.where((own_ids == shifted_ids)[:, None], actuators, jnp.zeros_like(actuators))
            return jnp.dot(masked.T, shifted, preferred_element_type=jnp.float32)
        products = lax.map(lag_product, shifts)
        return (running + products, None)
    initial = jnp.zeros((NBLK * LBW, M, P_SIZE), jnp.float32)
    summed, unused = lax.scan(add_block, initial, (actuator_blocks, sensor_blocks, next_heads, jnp.arange(blocks, dtype=jnp.int32)))
    return jnp.transpose(summed, (1, 0, 2)) * (1.0 / math.sqrt(sample_count))
```

```python
import math

import jax
import jax.numpy as jnp
from jax import lax
from jax.sharding import PartitionSpec as P

LMAX = 1024
LBW = 2
NBLK = 2
FINE = 64.0
FULL = 32766.0
LEAST = -112.0 * FINE
SCALE_ROWS = 8


def shifted_by(value, axis, steps):
    count = lax.axis_size(axis)
    initial, last = (max(0, -steps), min(count, count - steps))
    return lax.ppermute(value, axis, [(source, source + steps) for source in range(initial, last)])


def segment_ids(run_lengths, start_row, row_count):
    run_ends = jnp.cumsum(run_lengths)
    places = start_row + jnp.arange(row_count, dtype=jnp.int32)
    return jnp.sum((run_ends[None, :] <= places[:, None]).astype(jnp.int32), axis=1)


def product_over_time(masked, shifted):
    return lax.dot_general(
        masked, shifted, (((0,), (0,)), ((), ())), preferred_element_type=jnp.float32
    )


def per_device_plain(actuator_input, sensor_output, run_lengths, lag_offsets):
    samples = actuator_input.shape[0]
    devices_seg = lax.axis_size("seg")
    scaling = 1.0 / math.sqrt(samples * devices_seg)
    start_row = lax.axis_index("seg") * samples
    halo_rows = shifted_by(sensor_output[:LMAX], "seg", -1)
    idents = segment_ids(run_lengths, start_row, samples + LMAX)
    own_ids = idents[:samples]
    shifts = [lag_offsets[blk_num] + lag_step for blk_num in range(NBLK) for lag_step in range(LBW)]
    joined = jnp.concatenate([sensor_output, halo_rows], axis=0)

    def lag_term(lag_value):
        shifted = lax.dynamic_slice_in_dim(joined, lag_value, samples, 0)
        shifted_ids = lax.dynamic_slice_in_dim(idents, lag_value, samples, 0)
        masked = jnp.where((own_ids == shifted_ids)[:, None], actuator_input, jnp.zeros_like(actuator_input))
        return product_over_time(masked, shifted)

    shares = lax.psum_scatter(
        jnp.stack([lag_term(lag_value) for lag_value in shifts], axis=1),
        "seg",
        scatter_dimension=0,
        tiled=True,
    )
    result_rows = lax.all_to_all(shares, "lag", split_axis=1, concat_axis=2, tiled=True)
    return result_rows * scaling


def coded(value):
    largest = jnp.max(jnp.abs(value), axis=-2, keepdims=True)
    code = jnp.maximum(jnp.ceil(jnp.log2(largest) * FINE), LEAST)
    held = jnp.round(value * (jnp.exp2(code * (-1.0 / FINE)) * FULL))
    return held.astype(jnp.int32).astype(jnp.int16), code.astype(jnp.int32).astype(jnp.int16)


def decoded(held, code):
    return held.astype(jnp.float32) * (jnp.exp2(code.astype(jnp.float32) * (1.0 / FINE)) * (1.0 / FULL))


def exchange(value, seg_bits, lag_bits):
    segs, lags = lax.axis_size("seg"), lax.axis_size("lag")
    pairs = [
        (s * lags + l, (s ^ seg_bits) * lags + (l ^ lag_bits)) for s in range(segs) for l in range(lags)
    ]
    return lax.ppermute(value, ("seg", "lag"), pairs)


def per_device_staged(actuator_input, sensor_output, run_lengths, lag_offsets):
    samples, actuators = actuator_input.shape
    sensors = sensor_output.shape[1]
    segs, lags = lax.axis_size("seg"), lax.axis_size("lag")
    far = segs // 2
    rows = actuators // segs
    scaling = 1.0 / math.sqrt(samples * segs)
    seg, lag = lax.axis_index("seg"), lax.axis_index("lag")
    near_at, far_at = seg % 2, seg // 2
    start_row = seg * samples

    half = LMAX // 2
    core = lag % 2
    fetched = shifted_by(
        lax.dynamic_slice_in_dim(actuator_input, samples - LMAX + half * core, half, 0), "seg", 1
    )
    others = exchange(fetched, 0, 1)
    tail = jnp.where(
        core == 0,
        jnp.concatenate([fetched, others], axis=0),
        jnp.concatenate([others, fetched], axis=0),
    )

    idents = segment_ids(run_lengths, start_row - LMAX, samples + LMAX)
    own_ids = idents[LMAX:]
    offsets = lag_offsets[:, None] + jnp.arange(LBW, dtype=jnp.int32)[None, :]
    shifts = offsets.reshape(-1)
    blank = jnp.zeros((LMAX, actuators), actuator_input.dtype)
    inner = jnp.concatenate([blank, actuator_input], axis=0)
    outer = jnp.concatenate([tail, blank], axis=0)

    def product(step):
        lag_value = lax.dynamic_index_in_dim(shifts, lag ^ step, 0, keepdims=False)
        at = LMAX - lag_value
        same = own_ids == lax.dynamic_slice_in_dim(idents, at, samples, 0)

        def part(source, count):
            moved = lax.dynamic_slice_in_dim(source, at, count, 0)
            masked = jnp.where(same[:count, None], moved, jnp.zeros_like(moved))
            return product_over_time(masked, sensor_output[:count])

        whole = part(inner, samples) + part(outer, LMAX)
        return whole.reshape(far, 2, rows, sensors)

    def with_codes(held, code):
        return jnp.concatenate(
            [held, jnp.broadcast_to(code, (SCALE_ROWS, sensors))], axis=0
        )

    order = sorted(range(lags), key=lambda j: (j == 0, j % 2, -j))
    sums = [None] * lags
    kept = [None] * lags
    came = [None] * lags
    for step in order:
        terms = product(step)
        send = jnp.where(near_at == 0, terms[:, 1], terms[:, 0]).reshape(far * rows, sensors)
        own = jnp.where(near_at == 0, terms[:, 0], terms[:, 1]).reshape(far * rows, sensors)
        came[step] = exchange(with_codes(*coded(send)), 1, step)
        if step:
            kept[step] = exchange(with_codes(*coded(own)), 0, step)
        else:
            kept[step] = own

    def opened(payload):
        return decoded(payload[: far * rows], payload[far * rows : far * rows + 1])

    for step in range(lags):
        first = opened(kept[step]) if step else kept[step]
        sums[step] = (first + opened(came[step])).reshape(far, rows, sensors)
    stacked = jnp.stack(sums, axis=1)

    total = lax.dynamic_index_in_dim(stacked, far_at, 0, keepdims=False)
    for bits in range(1, far):
        block = lax.dynamic_index_in_dim(stacked, far_at ^ bits, 0, keepdims=False)
        held, code = coded(block)
        payload = jnp.concatenate(
            [
                held.reshape(lags * rows, sensors),
                code.reshape(lags, sensors),
                jnp.zeros((-lags % SCALE_ROWS, sensors), jnp.int16),
            ],
            axis=0,
        )
        payload = exchange(payload, 2 * bits, 0)
        total = total + decoded(
            payload[: lags * rows].reshape(lags, rows, sensors),
            payload[lags * rows : lags * rows + lags].reshape(lags, 1, sensors),
        )
    total = total * scaling
    bit = 1
    while bit < lags:
        turned = jnp.stack([total[place ^ bit] for place in range(lags)], axis=0)
        total = jnp.where((lag & bit) != 0, turned, total)
        bit *= 2
    return jnp.transpose(total, (1, 0, 2)).reshape(rows, 1, lags * sensors)


def solution(mesh):
    segs, lags = mesh.shape["seg"], mesh.shape["lag"]

    def per_device(actuator_input, sensor_output, run_lengths, lag_offsets):
        rows = actuator_input.shape[1] // segs
        staged = (
            4 <= segs <= 16
            and segs & (segs - 1) == 0
            and lags & (lags - 1) == 0
            and lags == NBLK * LBW
            and rows % 8 == 0
            and actuator_input.shape[0] >= LMAX
        )
        chosen = per_device_staged if staged else per_device_plain
        return chosen(actuator_input, sensor_output, run_lengths, lag_offsets)

    return jax.shard_map(
        per_device,
        mesh=mesh,
        in_specs=(P("seg", None), P("seg", "lag"), P(), P()),
        out_specs=P("seg", "lag", None),
        check_vma=False,
    )
```

```python
import math

import jax
import jax.numpy as jnp
from jax import lax
from jax.experimental import pallas as pl
from jax.experimental.pallas import tpu as pltpu
from jax.experimental import pallas as pl
from jax.experimental.pallas import tpu as pltpu
from jax.experimental import pallas as pl
from jax.experimental.pallas import tpu as pltpu
from jax.experimental import pallas as pl
from jax.experimental.pallas import tpu as pltpu
from jax.experimental import pallas as pl
from jax.experimental.pallas import tpu as pltpu
from jax.sharding import PartitionSpec as P


LMAX = 1024
LBW = 2
NBLK = 2
FINE = 64.0
FULL = 32700.0
LEAST = -112.0 * FINE
SCALE_ROWS = 8
LANES = 128
LANES = 128
LANES = 128
LANES = 128
LANES = 128


def shifted_by(value, axis, steps):
    count = lax.axis_size(axis)
    initial, last = (max(0, -steps), min(count, count - steps))
    return lax.ppermute(value, axis, [(source, source + steps) for source in range(initial, last)])


def segment_ids(run_lengths, start_row, row_count):
    run_ends = jnp.cumsum(run_lengths)
    places = start_row + jnp.arange(row_count, dtype=jnp.int32)
    return jnp.sum((run_ends[None, :] <= places[:, None]).astype(jnp.int32), axis=1)


def product_over_time(masked, shifted):
    return lax.dot_general(
        masked, shifted, (((0,), (0,)), ((), ())), preferred_element_type=jnp.float32
    )


def per_device_plain(actuator_input, sensor_output, run_lengths, lag_offsets):
    samples = actuator_input.shape[0]
    devices_seg = lax.axis_size("seg")
    scaling = 1.0 / math.sqrt(samples * devices_seg)
    start_row = lax.axis_index("seg") * samples
    halo_rows = shifted_by(sensor_output[:LMAX], "seg", -1)
    idents = segment_ids(run_lengths, start_row, samples + LMAX)
    own_ids = idents[:samples]
    shifts = [lag_offsets[blk_num] + lag_step for blk_num in range(NBLK) for lag_step in range(LBW)]
    joined = jnp.concatenate([sensor_output, halo_rows], axis=0)

    def lag_term(lag_value):
        shifted = lax.dynamic_slice_in_dim(joined, lag_value, samples, 0)
        shifted_ids = lax.dynamic_slice_in_dim(idents, lag_value, samples, 0)
        masked = jnp.where((own_ids == shifted_ids)[:, None], actuator_input, jnp.zeros_like(actuator_input))
        return product_over_time(masked, shifted)

    shares = lax.psum_scatter(
        jnp.stack([lag_term(lag_value) for lag_value in shifts], axis=1),
        "seg",
        scatter_dimension=0,
        tiled=True,
    )
    result_rows = lax.all_to_all(shares, "lag", split_axis=1, concat_axis=2, tiled=True)
    return result_rows * scaling


def exchange(value, seg_bits, lag_bits):
    segs, lags = lax.axis_size("seg"), lax.axis_size("lag")
    pairs = [
        (s * lags + l, (s ^ seg_bits) * lags + (l ^ lag_bits)) for s in range(segs) for l in range(lags)
    ]
    return lax.ppermute(value, ("seg", "lag"), pairs)


def column_code(largest):
    return jnp.maximum(jnp.ceil(jnp.log2(largest) * FINE), LEAST)


def coded(value, code):
    held = jnp.round(value * (jnp.exp2(code * (-1.0 / FINE)) * FULL))
    return held.astype(jnp.int32).astype(jnp.int16)


def decoded(held, code):
    return held.astype(jnp.float32) * (jnp.exp2(code * (1.0 / FINE)) * (1.0 / FULL))


def codes_of(ref, at):
    return ref[pl.ds(at, SCALE_ROWS), :].astype(jnp.int32).astype(jnp.float32)


def lag_of(offsets_ref, which):
    return offsets_ref[which // LBW] + which % LBW


def fill_rows(turned, at_lane, masked, at_masked, runs, offsets, lag, lags, start_row, chunk):
    actuators = turned.shape[0]
    tiles = chunk // LANES
    lane = lax.broadcasted_iota(jnp.int32, (1, LANES), 1)
    ends, end = [], jnp.int32(0)
    for run in range(runs.shape[0]):
        end = end + runs[run]
        ends.append(end)
    for step in range(lags):
        shift = lag_of(offsets, lag ^ step)
        at = at_lane - shift
        base, turn = at // LANES, at % LANES
        low = jnp.broadcast_to(lane < LANES - turn, (actuators, LANES))
        pieces = [
            pltpu.roll(
                turned[:, pl.ds(pl.multiple_of((base + tile) * LANES, LANES), LANES)],
                (LANES - turn) % LANES,
                1,
            )
            for tile in range(tiles + 1)
        ]
        for tile in range(tiles):
            place = lane + (start_row + tile * LANES)
            crossed = jnp.zeros((1, LANES), jnp.int32)
            for end in ends:
                crossed = crossed + ((end <= place) & (end > place - shift)).astype(jnp.int32)
            keep = jnp.broadcast_to(crossed == 0, (actuators, LANES))
            value = jnp.where(low, pieces[tile], pieces[tile + 1])
            value = jnp.where(keep, value, jnp.zeros_like(value))
            masked[pl.ds(step * actuators, actuators), pl.ds(at_masked + tile * LANES, LANES)] = value


def inner_kernel(
    runs_ref, offsets_ref, actuators_ref, sensors_ref, out_ref, runs, offsets, held, sensed, turned, masked, sems
):
    chunk, lags = LMAX, lax.axis_size("lag")
    samples, _ = actuators_ref.shape
    chunks = samples // chunk
    copies = [
        pltpu.make_async_copy(runs_ref, runs, sems.at[0]),
        pltpu.make_async_copy(offsets_ref, offsets, sems.at[1]),
    ]
    for at in range(chunks):
        here = pl.ds(at * chunk, chunk)
        copies.append(pltpu.make_async_copy(actuators_ref.at[here, :], held.at[here, :], sems.at[2 + at]))
    for at in range(1, chunks):
        copies.append(
            pltpu.make_async_copy(
                sensors_ref.at[pl.ds(at * chunk, chunk), :],
                sensed.at[pl.ds((at - 1) * chunk, chunk), :],
                sems.at[1 + chunks + at],
            )
        )
    for copy in copies:
        copy.start()
    start_row = lax.axis_index("seg") * samples
    for at in range(chunks):
        copies[2 + at].wait()
        here = pl.ds(at * chunk, chunk)
        turned[:, here] = held[here, :].T
        if at == 0:
            copies[0].wait()
            copies[1].wait()
            continue
        fill_rows(
            turned, at * chunk, masked, (at - 1) * chunk, runs, offsets,
            lax.axis_index("lag"), lags, start_row + at * chunk, chunk,
        )
        copies[1 + chunks + at].wait()
        there = pl.ds((at - 1) * chunk, chunk)
        terms = jnp.dot(masked[:, there], sensed[there, :], preferred_element_type=jnp.float32)
        if at == 1:
            out_ref[...] = terms
        else:
            out_ref[...] += terms


def outer_kernel(
    runs_ref, offsets_ref, mine_ref, theirs_ref, actuators_ref, sensors_ref, inner_ref, *refs
):
    chunk, lags, segs = LMAX, lax.axis_size("lag"), lax.axis_size("seg")
    sends, keeps, own_ref = refs[:lags], (None,) + refs[lags : 2 * lags - 1], refs[2 * lags - 1]
    runs, offsets, held, sensed, turned, masked, terms, sems = refs[2 * lags :]
    samples, actuators = actuators_ref.shape
    here = pl.ds(0, chunk)
    copies = [
        pltpu.make_async_copy(actuators_ref.at[here, :], held, sems.at[2]),
        pltpu.make_async_copy(runs_ref, runs, sems.at[0]),
        pltpu.make_async_copy(offsets_ref, offsets, sems.at[1]),
        pltpu.make_async_copy(sensors_ref.at[here, :], sensed, sems.at[3]),
    ]
    for copy in copies:
        copy.start()
    seg, lag = lax.axis_index("seg"), lax.axis_index("lag")
    rows, far, half = actuators // segs, segs // 2, chunk // 2
    core = lag % 2
    turned[:, pl.ds(pl.multiple_of(core * half, LANES), half)] = mine_ref[...].T
    turned[:, pl.ds(pl.multiple_of((1 - core) * half, LANES), half)] = theirs_ref[...].T
    copies[0].wait()
    turned[:, pl.ds(chunk, chunk)] = held[...].T
    copies[1].wait()
    copies[2].wait()
    fill_rows(turned, chunk, masked, 0, runs, offsets, lag, lags, seg * samples, chunk)
    copies[3].wait()
    terms[...] = inner_ref[...] + jnp.dot(masked[...], sensed[...], preferred_element_type=jnp.float32)

    def half_of(step, near):
        return [
            terms[pl.ds(pl.multiple_of(step * actuators + (2 * block + near) * rows, rows), rows), :]
            for block in range(far)
        ]

    def send(step, near, ref):
        parts = half_of(step, near)
        largest = jnp.abs(parts[0])
        for part in parts[1:]:
            largest = jnp.maximum(largest, jnp.abs(part))
        code = column_code(jnp.max(largest, axis=0, keepdims=True))
        for block, part in enumerate(parts):
            ref[pl.ds(block * rows, rows), :] = coded(part, code)
        ref[pl.ds(far * rows, SCALE_ROWS), :] = jnp.broadcast_to(
            code.astype(jnp.int32), (SCALE_ROWS, code.shape[1])
        ).astype(jnp.int16)

    near_at = seg % 2
    for step in range(lags):
        send(step, 1 - near_at, sends[step])
        if step:
            send(step, near_at, keeps[step])
        else:
            for block, part in enumerate(half_of(step, near_at)):
                own_ref[pl.ds(block * rows, rows), :] = part


def middle_kernel(*refs):
    lags, segs = lax.axis_size("lag"), lax.axis_size("seg")
    far = segs // 2
    came, kept, own_ref = refs[:lags], (None,) + refs[lags : 2 * lags - 1], refs[2 * lags - 1]
    total_ref, sends = refs[2 * lags], refs[2 * lags + 1 :]
    rows = total_ref.shape[0] // lags
    far_at = lax.axis_index("seg") // 2
    came_codes = [codes_of(ref, far * rows)[:1] for ref in came]
    kept_codes = [None] + [codes_of(ref, far * rows)[:1] for ref in kept[1:]]

    def block_sum(step, block):
        here = pl.ds(pl.multiple_of(block * rows, rows), rows)
        first = own_ref[here, :] if step == 0 else decoded(kept[step][here, :], kept_codes[step])
        return first + decoded(came[step][here, :], came_codes[step])

    for step in range(lags):
        total_ref[pl.ds(step * rows, rows), :] = block_sum(step, far_at)
    sublane = lax.broadcasted_iota(jnp.int32, (SCALE_ROWS, total_ref.shape[1]), 0)
    for bits in range(1, far):
        codes = jnp.zeros(sublane.shape, jnp.int32)
        for step in range(lags):
            part = block_sum(step, far_at ^ bits)
            code = column_code(jnp.max(jnp.abs(part), axis=0, keepdims=True))
            sends[bits - 1][pl.ds(step * rows, rows), :] = coded(part, code)
            codes = jnp.where(sublane == step, jnp.broadcast_to(code.astype(jnp.int32), sublane.shape), codes)
        sends[bits - 1][pl.ds(lags * rows, SCALE_ROWS), :] = codes.astype(jnp.int16)


def last_kernel(scaling, total_ref, *refs):
    lags = lax.axis_size("lag")
    came, out_ref = refs[:-1], refs[-1]
    rows = total_ref.shape[0] // lags
    width = total_ref.shape[1]
    lag = lax.axis_index("lag")
    codes = [codes_of(ref, lags * rows) for ref in came]
    for step in range(lags):
        here = pl.ds(step * rows, rows)
        value = total_ref[here, :]
        for ref, code in zip(came, codes):
            value = value + decoded(ref[here, :], code[step : step + 1])
        out_ref[:, 0, pl.ds(pl.multiple_of((lag ^ step) * width, LANES), width)] = value * scaling


def per_device_staged(actuator_input, sensor_output, run_lengths, lag_offsets):
    samples, actuators = actuator_input.shape
    sensors = sensor_output.shape[1]
    segs, lags = lax.axis_size("seg"), lax.axis_size("lag")
    far, rows, chunk = segs // 2, actuators // segs, LMAX
    scaling = 1.0 / math.sqrt(samples * segs)
    lag = lax.axis_index("lag")
    spare = lags * actuators
    payload = jax.ShapeDtypeStruct((far * rows + SCALE_ROWS, sensors), jnp.int16)
    onward = jax.ShapeDtypeStruct((lags * rows + SCALE_ROWS, sensors), jnp.int16)
    vmem = pl.BlockSpec(memory_space=pltpu.VMEM)
    half = LMAX // 2
    core = lag % 2
    fetched = shifted_by(
        lax.dynamic_slice_in_dim(actuator_input, samples - LMAX + half * core, half, 0), "seg", 1
    )
    others = exchange(fetched, 0, 1)

    hbm = pl.BlockSpec(memory_space=pltpu.HBM)
    scalars = [pltpu.SMEM(run_lengths.shape, jnp.int32), pltpu.SMEM(lag_offsets.shape, jnp.int32)]
    chunks = samples // chunk
    inner = pl.pallas_call(
        inner_kernel,
        in_specs=[hbm] * 4,
        out_specs=vmem,
        out_shape=jax.ShapeDtypeStruct((spare, sensors), jnp.float32),
        scratch_shapes=scalars
        + [
            pltpu.VMEM((samples, actuators), jnp.bfloat16),
            pltpu.VMEM((samples - chunk, sensors), jnp.bfloat16),
            pltpu.VMEM((actuators, samples + LANES), jnp.bfloat16),
            pltpu.VMEM((spare, samples - chunk), jnp.bfloat16),
            pltpu.SemaphoreType.DMA((1 + 2 * chunks,)),
        ],
        compiler_params=pltpu.CompilerParams(vmem_limit_bytes=48 << 20),
        cost_estimate=pl.CostEstimate(
            flops=2 * spare * sensors * (samples - chunk), bytes_accessed=6 << 20, transcendentals=0
        ),
        name="inner",
    )(run_lengths, lag_offsets, actuator_input, sensor_output)

    packed = pl.pallas_call(
        outer_kernel,
        in_specs=[hbm] * 2 + [vmem] * 2 + [hbm] * 2 + [vmem],
        out_specs=[vmem] * (2 * lags),
        out_shape=[payload] * (2 * lags - 1) + [jax.ShapeDtypeStruct((far * rows, sensors), jnp.float32)],
        scratch_shapes=scalars
        + [
            pltpu.VMEM((chunk, actuators), jnp.bfloat16),
            pltpu.VMEM((chunk, sensors), jnp.bfloat16),
            pltpu.VMEM((actuators, 2 * chunk + LANES), jnp.bfloat16),
            pltpu.VMEM((spare, chunk), jnp.bfloat16),
            pltpu.VMEM((spare, sensors), jnp.float32),
            pltpu.SemaphoreType.DMA((4,)),
        ],
        compiler_params=pltpu.CompilerParams(vmem_limit_bytes=48 << 20),
        cost_estimate=pl.CostEstimate(
            flops=2 * spare * sensors * chunk, bytes_accessed=6 << 20, transcendentals=0
        ),
        name="outer",
    )(run_lengths, lag_offsets, fetched, others, actuator_input, sensor_output, inner)

    came, kept = [None] * lags, [None] * lags
    for place in range(lags // 2):
        low, high = (place + 1) % (lags // 2), lags // 2 + place
        came[low] = exchange(packed[low], 1, low)
        kept[high] = exchange(packed[lags + high - 1], 0, high)
        came[high] = exchange(packed[high], 1, high)
    for step in range(1, lags // 2):
        kept[step] = exchange(packed[lags + step - 1], 0, step)

    middle = pl.pallas_call(
        middle_kernel,
        in_specs=[vmem] * (2 * lags),
        out_specs=[vmem] * far,
        out_shape=[jax.ShapeDtypeStruct((lags * rows, sensors), jnp.float32)] + [onward] * (far - 1),
        compiler_params=pltpu.CompilerParams(vmem_limit_bytes=8 << 20),
        name="middle",
    )(*came, *kept[1:], packed[-1])

    arrived = [exchange(middle[bits], 2 * bits, 0) for bits in range(far - 1, 0, -1)][::-1]

    def last_body(*refs):
        return last_kernel(scaling, *refs)

    return pl.pallas_call(
        last_body,
        in_specs=[vmem] * far,
        out_specs=vmem,
        out_shape=jax.ShapeDtypeStruct((rows, 1, lags * sensors), jnp.float32),
        compiler_params=pltpu.CompilerParams(vmem_limit_bytes=8 << 20),
        name="last",
    )(middle[0], *arrived)


def solution(mesh):
    segs, lags = mesh.shape["seg"], mesh.shape["lag"]

    def per_device(actuator_input, sensor_output, run_lengths, lag_offsets):
        rows = actuator_input.shape[1] // segs
        staged = (
            4 <= segs <= 16
            and segs & (segs - 1) == 0
            and lags & (lags - 1) == 0
            and lags == NBLK * LBW
            and rows % 8 == 0
            and actuator_input.shape[0] % LMAX == 0
            and actuator_input.shape[0] > LMAX
        )
        chosen = per_device_staged if staged else per_device_plain
        return chosen(actuator_input, sensor_output, run_lengths, lag_offsets)

    mapped = jax.shard_map(
        per_device,
        mesh=mesh,
        in_specs=(P("seg", None), P("seg", "lag"), P(), P()),
        out_specs=P("seg", "lag", None),
        check_vma=False,
    )
    return mapped
    return mapped
    return mapped
    return mapped
```

```python
import math

import jax
import jax.numpy as jnp
from jax import lax
from jax.experimental import pallas as pl
from jax.experimental.pallas import tpu as pltpu
from jax.experimental import pallas as pl
from jax.experimental.pallas import tpu as pltpu
from jax.experimental import pallas as pl
from jax.experimental.pallas import tpu as pltpu
from jax.experimental import pallas as pl
from jax.experimental.pallas import tpu as pltpu
from jax.experimental import pallas as pl
from jax.experimental.pallas import tpu as pltpu
from jax.experimental import pallas as pl
from jax.experimental.pallas import tpu as pltpu
from jax.experimental import pallas as pl
from jax.experimental.pallas import tpu as pltpu
from jax.sharding import PartitionSpec as P


LMAX = 1024
LBW = 2
NBLK = 2
FINE = 64.0
FULL = 32700.0
LEAST = -112.0 * FINE
SCALE_ROWS = 8
LANES = 128
LANES = 128
LANES = 128
LANES = 128
LANES = 128
LANES = 128
LANES = 128


def shifted_by(value, axis, steps):
    count = lax.axis_size(axis)
    initial, last = (max(0, -steps), min(count, count - steps))
    return lax.ppermute(value, axis, [(source, source + steps) for source in range(initial, last)])


def segment_ids(run_lengths, start_row, row_count):
    run_ends = jnp.cumsum(run_lengths)
    places = start_row + jnp.arange(row_count, dtype=jnp.int32)
    return jnp.sum((run_ends[None, :] <= places[:, None]).astype(jnp.int32), axis=1)


def product_over_time(masked, shifted):
    return lax.dot_general(
        masked, shifted, (((0,), (0,)), ((), ())), preferred_element_type=jnp.float32
    )


def per_device_plain(actuator_input, sensor_output, run_lengths, lag_offsets):
    samples = actuator_input.shape[0]
    devices_seg = lax.axis_size("seg")
    scaling = 1.0 / math.sqrt(samples * devices_seg)
    start_row = lax.axis_index("seg") * samples
    halo_rows = shifted_by(sensor_output[:LMAX], "seg", -1)
    idents = segment_ids(run_lengths, start_row, samples + LMAX)
    own_ids = idents[:samples]
    shifts = [lag_offsets[blk_num] + lag_step for blk_num in range(NBLK) for lag_step in range(LBW)]
    joined = jnp.concatenate([sensor_output, halo_rows], axis=0)

    def lag_term(lag_value):
        shifted = lax.dynamic_slice_in_dim(joined, lag_value, samples, 0)
        shifted_ids = lax.dynamic_slice_in_dim(idents, lag_value, samples, 0)
        masked = jnp.where((own_ids == shifted_ids)[:, None], actuator_input, jnp.zeros_like(actuator_input))
        return product_over_time(masked, shifted)

    shares = lax.psum_scatter(
        jnp.stack([lag_term(lag_value) for lag_value in shifts], axis=1),
        "seg",
        scatter_dimension=0,
        tiled=True,
    )
    result_rows = lax.all_to_all(shares, "lag", split_axis=1, concat_axis=2, tiled=True)
    return result_rows * scaling


def exchange(value, seg_bits, lag_bits):
    segs, lags = lax.axis_size("seg"), lax.axis_size("lag")
    pairs = [
        (s * lags + l, (s ^ seg_bits) * lags + (l ^ lag_bits)) for s in range(segs) for l in range(lags)
    ]
    return lax.ppermute(value, ("seg", "lag"), pairs)


def column_code(largest):
    return jnp.maximum(jnp.ceil(jnp.log2(largest) * FINE), LEAST)


def coded(value, code):
    held = jnp.round(value * (jnp.exp2(code * (-1.0 / FINE)) * FULL))
    return held.astype(jnp.int32).astype(jnp.int16)


def decoded(held, code):
    return held.astype(jnp.float32) * (jnp.exp2(code * (1.0 / FINE)) * (1.0 / FULL))


def codes_of(ref, at):
    return ref[pl.ds(at, SCALE_ROWS), :].astype(jnp.int32).astype(jnp.float32)


def lag_of(offsets_ref, which):
    return offsets_ref[which // LBW] + which % LBW


def fill_rows(turned, at_lane, masked, at_masked, runs, offsets, lag, lags, start_row, chunk):
    actuators = turned.shape[0]
    tiles = chunk // LANES
    lane = lax.broadcasted_iota(jnp.int32, (1, LANES), 1)
    ends, end = [], jnp.int32(0)
    for run in range(runs.shape[0]):
        end = end + runs[run]
        ends.append(end)
    for step in range(lags):
        shift = lag_of(offsets, lag ^ step)
        at = at_lane - shift
        base, turn = at // LANES, at % LANES
        low = jnp.broadcast_to(lane < LANES - turn, (actuators, LANES))
        pieces = [
            pltpu.roll(
                turned[:, pl.ds(pl.multiple_of((base + tile) * LANES, LANES), LANES)],
                (LANES - turn) % LANES,
                1,
            )
            for tile in range(tiles + 1)
        ]
        for tile in range(tiles):
            place = lane + (start_row + tile * LANES)
            crossed = jnp.zeros((1, LANES), jnp.int32)
            for end in ends:
                crossed = crossed + ((end <= place) & (end > place - shift)).astype(jnp.int32)
            keep = jnp.broadcast_to(crossed == 0, (actuators, LANES))
            value = jnp.where(low, pieces[tile], pieces[tile + 1])
            value = jnp.where(keep, value, jnp.zeros_like(value))
            masked[pl.ds(step * actuators, actuators), pl.ds(at_masked + tile * LANES, LANES)] = value


def inner_kernel(
    runs_ref, offsets_ref, actuators_ref, sensors_ref, out_ref, runs, offsets, held, sensed, turned, masked, sems
):
    chunk, lags = LMAX, lax.axis_size("lag")
    samples, _ = actuators_ref.shape
    chunks = samples // chunk
    copies = [
        pltpu.make_async_copy(runs_ref, runs, sems.at[0]),
        pltpu.make_async_copy(offsets_ref, offsets, sems.at[1]),
    ]
    for at in range(chunks):
        here = pl.ds(at * chunk, chunk)
        copies.append(pltpu.make_async_copy(actuators_ref.at[here, :], held.at[here, :], sems.at[2 + at]))
    for at in range(1, chunks):
        copies.append(
            pltpu.make_async_copy(
                sensors_ref.at[pl.ds(at * chunk, chunk), :],
                sensed.at[pl.ds((at - 1) * chunk, chunk), :],
                sems.at[1 + chunks + at],
            )
        )
    for copy in copies:
        copy.start()
    start_row = lax.axis_index("seg") * samples
    for at in range(chunks):
        copies[2 + at].wait()
        here = pl.ds(at * chunk, chunk)
        turned[:, here] = held[here, :].T
        if at == 0:
            copies[0].wait()
            copies[1].wait()
            continue
        fill_rows(
            turned, at * chunk, masked, (at - 1) * chunk, runs, offsets,
            lax.axis_index("lag"), lags, start_row + at * chunk, chunk,
        )
        copies[1 + chunks + at].wait()
        there = pl.ds((at - 1) * chunk, chunk)
        terms = jnp.dot(masked[:, there], sensed[there, :], preferred_element_type=jnp.float32)
        if at == 1:
            out_ref[...] = terms
        else:
            out_ref[...] += terms


def cut_kernel(actuators_ref, out_ref, sem):
    half = out_ref.shape[0]
    start = actuators_ref.shape[0] - LMAX + half * (lax.axis_index("lag") % 2)
    copy = pltpu.make_async_copy(actuators_ref.at[pl.ds(pl.multiple_of(start, 8), half), :], out_ref, sem)
    copy.start()
    copy.wait()


def outer_kernel(
    runs_ref, offsets_ref, mine_ref, theirs_ref, actuators_ref, sensors_ref, inner_ref,
    near_ref, near_own_ref, far_own_ref, *refs
):
    chunk, lags, segs = LMAX, lax.axis_size("lag"), lax.axis_size("seg")
    far = segs // 2
    far_refs = (None,) + refs[: far - 1]
    runs, offsets, held, sensed, turned, masked, terms, sems = refs[far - 1 :]
    samples, actuators = actuators_ref.shape
    here = pl.ds(0, chunk)
    copies = [
        pltpu.make_async_copy(actuators_ref.at[here, :], held, sems.at[2]),
        pltpu.make_async_copy(runs_ref, runs, sems.at[0]),
        pltpu.make_async_copy(offsets_ref, offsets, sems.at[1]),
        pltpu.make_async_copy(sensors_ref.at[here, :], sensed, sems.at[3]),
    ]
    for copy in copies:
        copy.start()
    seg, lag = lax.axis_index("seg"), lax.axis_index("lag")
    rows, half = actuators // segs, chunk // 2
    core = lag % 2
    turned[:, pl.ds(pl.multiple_of(core * half, LANES), half)] = mine_ref[...].T
    turned[:, pl.ds(pl.multiple_of((1 - core) * half, LANES), half)] = theirs_ref[...].T
    copies[0].wait()
    turned[:, pl.ds(chunk, chunk)] = held[...].T
    copies[1].wait()
    copies[2].wait()
    fill_rows(turned, chunk, masked, 0, runs, offsets, lag, lags, seg * samples, chunk)
    copies[3].wait()
    terms[...] = inner_ref[...] + jnp.dot(masked[...], sensed[...], preferred_element_type=jnp.float32)

    near_at, far_at = seg % 2, seg // 2

    def block_of(step, block, near, count):
        start = step * actuators + (2 * block + near) * rows
        return terms[pl.ds(pl.multiple_of(start, rows), count), :]

    codes = []
    for step in range(1, lags):
        parts = [block_of(step, block, 1 - near_at, rows) for block in range(far)]
        codes.append(put(near_ref, (step - 1) * far * rows, parts))
        for block in range(far):
            near_own_ref[pl.ds(((step - 1) * far + block) * rows, rows), :] = block_of(step, block, near_at, rows)
    put_codes(near_ref, (lags - 1) * far * rows, codes)
    for bits in range(1, far):
        code = put(far_refs[bits], 0, [block_of(0, far_at ^ bits, 0, 2 * rows)])
        put_codes(far_refs[bits], 2 * rows, [code])
    far_own_ref[...] = block_of(0, far_at, 0, 2 * rows)


def put(ref, at, parts):
    largest = jnp.abs(parts[0])
    for part in parts[1:]:
        largest = jnp.maximum(largest, jnp.abs(part))
    code = column_code(jnp.max(largest, axis=0, keepdims=True))
    for part in parts:
        ref[pl.ds(at, part.shape[0]), :] = coded(part, code)
        at += part.shape[0]
    return code


def put_codes(ref, at, codes):
    shape = (SCALE_ROWS, codes[0].shape[1])
    sublane = lax.broadcasted_iota(jnp.int32, shape, 0)
    rows = jnp.broadcast_to(codes[0].astype(jnp.int32), shape)
    for row in range(1, len(codes)):
        rows = jnp.where(sublane == row, jnp.broadcast_to(codes[row].astype(jnp.int32), shape), rows)
    ref[pl.ds(at, SCALE_ROWS), :] = rows.astype(jnp.int16)


def second_kernel(came_ref, near_own_ref, far_own_ref, *refs):
    lags, segs = lax.axis_size("lag"), lax.axis_size("seg")
    far, others = segs // 2, lags - 1
    came_far = (None,) + refs[: far - 1]
    total_ref, own_ref, near_ref = refs[far - 1 : far + 2]
    far_refs = (None,) + refs[far + 2 :]
    rows = own_ref.shape[0]
    near_at, far_at = lax.axis_index("seg") % 2, lax.axis_index("seg") // 2
    came_codes = codes_of(came_ref, others * far * rows)

    def block_sum(step, block):
        here = pl.ds(pl.multiple_of((step * far + block) * rows, rows), rows)
        return near_own_ref[here, :] + decoded(came_ref[here, :], came_codes[step : step + 1])

    for bits in range(far - 1, 0, -1):
        codes = [
            put(far_refs[bits], step * rows, [block_sum(step, far_at ^ bits)]) for step in range(others)
        ]
        put_codes(far_refs[bits], others * rows, codes)
    far_codes = [None] + [codes_of(ref, 2 * rows)[:1] for ref in came_far[1:]]

    def near_sum(near):
        here = pl.ds(pl.multiple_of(near * rows, rows), rows)
        value = far_own_ref[here, :]
        for bits in range(1, far):
            value = value + decoded(came_far[bits][here, :], far_codes[bits])
        return value

    put_codes(near_ref, rows, [put(near_ref, 0, [near_sum(1 - near_at)])])
    own_ref[...] = near_sum(near_at)
    for step in range(others):
        total_ref[pl.ds(step * rows, rows), :] = block_sum(step, far_at)


def third_kernel(total_ref, *refs):
    lags, segs = lax.axis_size("lag"), lax.axis_size("seg")
    far = segs // 2
    came, sends = refs[: far - 1], refs[far - 1 :]
    rows = total_ref.shape[0] // (lags - 1)
    codes = [codes_of(ref, (lags - 1) * rows) for ref in came]
    for step in range(lags - 1):
        here = pl.ds(step * rows, rows)
        value = total_ref[here, :]
        for ref, code in zip(came, codes):
            value = value + decoded(ref[here, :], code[step : step + 1])
        put_codes(sends[step], rows, [put(sends[step], 0, [value])])


def last_kernel(scaling, own_ref, near_ref, *refs):
    came, out_ref = (None,) + refs[:-1], refs[-1]
    rows, width = own_ref.shape
    lag = lax.axis_index("lag")
    for step in range(len(came)):
        ref = came[step] if step else near_ref
        value = decoded(ref[pl.ds(0, rows), :], codes_of(ref, rows)[:1])
        if step == 0:
            value = value + own_ref[...]
        out_ref[:, 0, pl.ds(pl.multiple_of((lag ^ step) * width, LANES), width)] = value * scaling


def per_device_staged(actuator_input, sensor_output, run_lengths, lag_offsets):
    samples, actuators = actuator_input.shape
    sensors = sensor_output.shape[1]
    segs, lags = lax.axis_size("seg"), lax.axis_size("lag")
    far, rows, chunk = segs // 2, actuators // segs, LMAX
    scaling = 1.0 / math.sqrt(samples * segs)
    spare = lags * actuators
    others = lags - 1

    def payload(count):
        return jax.ShapeDtypeStruct((count * rows + SCALE_ROWS, sensors), jnp.int16)

    def wide(count):
        return jax.ShapeDtypeStruct((count * rows, sensors), jnp.float32)

    vmem = pl.BlockSpec(memory_space=pltpu.VMEM)
    small = pltpu.CompilerParams(vmem_limit_bytes=8 << 20)
    hbm = pl.BlockSpec(memory_space=pltpu.HBM)
    scalars = [pltpu.SMEM(run_lengths.shape, jnp.int32), pltpu.SMEM(lag_offsets.shape, jnp.int32)]
    chunks = samples // chunk
    run_lengths, lag_offsets, actuator_input, sensor_output = (
        pltpu.with_memory_space_constraint(value, pltpu.HBM)
        for value in (run_lengths, lag_offsets, actuator_input, sensor_output)
    )

    cut = pl.pallas_call(
        cut_kernel,
        in_specs=[hbm],
        out_specs=vmem,
        out_shape=jax.ShapeDtypeStruct((LMAX // 2, actuators), jnp.bfloat16),
        scratch_shapes=[pltpu.SemaphoreType.DMA],
        compiler_params=small,
        name="cut",
    )(actuator_input)
    fetched = shifted_by(cut, "seg", 1)
    swapped = exchange(fetched, 0, 1)

    inner = pl.pallas_call(
        inner_kernel,
        in_specs=[hbm] * 4,
        out_specs=vmem,
        out_shape=jax.ShapeDtypeStruct((spare, sensors), jnp.float32),
        scratch_shapes=scalars
        + [
            pltpu.VMEM((samples, actuators), jnp.bfloat16),
            pltpu.VMEM((samples - chunk, sensors), jnp.bfloat16),
            pltpu.VMEM((actuators, samples + LANES), jnp.bfloat16),
            pltpu.VMEM((spare, samples - chunk), jnp.bfloat16),
            pltpu.SemaphoreType.DMA((1 + 2 * chunks,)),
        ],
        compiler_params=pltpu.CompilerParams(vmem_limit_bytes=48 << 20),
        cost_estimate=pl.CostEstimate(
            flops=2 * spare * sensors * (samples - chunk), bytes_accessed=6 << 20, transcendentals=0
        ),
        name="inner",
    )(run_lengths, lag_offsets, actuator_input, sensor_output)

    packed = pl.pallas_call(
        outer_kernel,
        in_specs=[hbm] * 2 + [vmem] * 2 + [hbm] * 2 + [vmem],
        out_specs=[vmem] * (far + 2),
        out_shape=[payload(others * far), wide(others * far), wide(2)] + [payload(2)] * (far - 1),
        scratch_shapes=scalars
        + [
            pltpu.VMEM((chunk, actuators), jnp.bfloat16),
            pltpu.VMEM((chunk, sensors), jnp.bfloat16),
            pltpu.VMEM((actuators, 2 * chunk + LANES), jnp.bfloat16),
            pltpu.VMEM((spare, chunk), jnp.bfloat16),
            pltpu.VMEM((spare, sensors), jnp.float32),
            pltpu.SemaphoreType.DMA((4,)),
        ],
        compiler_params=pltpu.CompilerParams(vmem_limit_bytes=48 << 20),
        cost_estimate=pl.CostEstimate(
            flops=2 * spare * sensors * chunk, bytes_accessed=6 << 20, transcendentals=0
        ),
        name="outer",
    )(run_lengths, lag_offsets, fetched, swapped, actuator_input, sensor_output, inner)

    masks = range(far - 1, 0, -1)
    came = exchange(packed[0], 1, 0)
    came_far = [exchange(packed[2 + bits], 2 * bits, 0) for bits in masks][::-1]
    second = pl.pallas_call(
        second_kernel,
        in_specs=[vmem] * (far + 2),
        out_specs=[vmem] * (far + 2),
        out_shape=[wide(others), wide(1), payload(1)] + [payload(others)] * (far - 1),
        compiler_params=small,
        name="second",
    )(came, packed[1], packed[2], *came_far)
    came_far = [exchange(second[2 + bits], 2 * bits, 0) for bits in masks][::-1]
    near = exchange(second[2], 1, 0)
    third = pl.pallas_call(
        third_kernel,
        in_specs=[vmem] * far,
        out_specs=[vmem] * others,
        out_shape=[payload(1)] * others,
        compiler_params=small,
        name="third",
    )(second[0], *came_far)
    came = [exchange(third[step - 1], 0, step) for step in range(others, 0, -1)][::-1]

    def last_body(*refs):
        return last_kernel(scaling, *refs)

    return pl.pallas_call(
        last_body,
        in_specs=[vmem] * (2 + others),
        out_specs=vmem,
        out_shape=jax.ShapeDtypeStruct((rows, 1, lags * sensors), jnp.float32),
        compiler_params=small,
        name="last",
    )(second[1], near, *came)


def solution(mesh):
    segs, lags = mesh.shape["seg"], mesh.shape["lag"]

    def per_device(actuator_input, sensor_output, run_lengths, lag_offsets):
        rows = actuator_input.shape[1] // segs
        staged = (
            4 <= segs <= 16
            and segs & (segs - 1) == 0
            and lags & (lags - 1) == 0
            and lags == NBLK * LBW
            and rows % 8 == 0
            and actuator_input.shape[0] % LMAX == 0
            and actuator_input.shape[0] > LMAX
        )
        chosen = per_device_staged if staged else per_device_plain
        return chosen(actuator_input, sensor_output, run_lengths, lag_offsets)

    mapped = jax.shard_map(
        per_device,
        mesh=mesh,
        in_specs=(P("seg", None), P("seg", "lag"), P(), P()),
        out_specs=P("seg", "lag", None),
        check_vma=False,
    )
    return mapped
    return mapped
    return mapped
    return mapped
    return mapped
    return mapped
```

```python
import math

import jax
import jax.numpy as jnp
from jax import lax
from jax.experimental import pallas as pl
from jax.experimental.pallas import tpu as pltpu
from jax.experimental import pallas as pl
from jax.experimental.pallas import tpu as pltpu
from jax.experimental import pallas as pl
from jax.experimental.pallas import tpu as pltpu
from jax.experimental import pallas as pl
from jax.experimental.pallas import tpu as pltpu
from jax.experimental import pallas as pl
from jax.experimental.pallas import tpu as pltpu
from jax.experimental import pallas as pl
from jax.experimental.pallas import tpu as pltpu
from jax.experimental import pallas as pl
from jax.experimental.pallas import tpu as pltpu
from jax.sharding import PartitionSpec as P


LMAX = 1024
LBW = 2
NBLK = 2
FINE = 64.0
FULL = 32700.0
LEAST = -112.0 * FINE
SCALE_ROWS = 8
LANES = 128
LANES = 128
LANES = 128
LANES = 128
LANES = 128
LANES = 128
LANES = 128


def shifted_by(value, axis, steps):
    count = lax.axis_size(axis)
    initial, last = (max(0, -steps), min(count, count - steps))
    return lax.ppermute(value, axis, [(source, source + steps) for source in range(initial, last)])


def segment_ids(run_lengths, start_row, row_count):
    run_ends = jnp.cumsum(run_lengths)
    places = start_row + jnp.arange(row_count, dtype=jnp.int32)
    return jnp.sum((run_ends[None, :] <= places[:, None]).astype(jnp.int32), axis=1)


def product_over_time(masked, shifted):
    return lax.dot_general(
        masked, shifted, (((0,), (0,)), ((), ())), preferred_element_type=jnp.float32
    )


def per_device_plain(actuator_input, sensor_output, run_lengths, lag_offsets):
    samples = actuator_input.shape[0]
    devices_seg = lax.axis_size("seg")
    scaling = 1.0 / math.sqrt(samples * devices_seg)
    start_row = lax.axis_index("seg") * samples
    halo_rows = shifted_by(sensor_output[:LMAX], "seg", -1)
    idents = segment_ids(run_lengths, start_row, samples + LMAX)
    own_ids = idents[:samples]
    shifts = [lag_offsets[blk_num] + lag_step for blk_num in range(NBLK) for lag_step in range(LBW)]
    joined = jnp.concatenate([sensor_output, halo_rows], axis=0)

    def lag_term(lag_value):
        shifted = lax.dynamic_slice_in_dim(joined, lag_value, samples, 0)
        shifted_ids = lax.dynamic_slice_in_dim(idents, lag_value, samples, 0)
        masked = jnp.where((own_ids == shifted_ids)[:, None], actuator_input, jnp.zeros_like(actuator_input))
        return product_over_time(masked, shifted)

    shares = lax.psum_scatter(
        jnp.stack([lag_term(lag_value) for lag_value in shifts], axis=1),
        "seg",
        scatter_dimension=0,
        tiled=True,
    )
    result_rows = lax.all_to_all(shares, "lag", split_axis=1, concat_axis=2, tiled=True)
    return result_rows * scaling


def exchange(value, seg_bits, lag_bits):
    segs, lags = lax.axis_size("seg"), lax.axis_size("lag")
    pairs = [
        (s * lags + l, (s ^ seg_bits) * lags + (l ^ lag_bits)) for s in range(segs) for l in range(lags)
    ]
    return lax.ppermute(value, ("seg", "lag"), pairs)


def column_code(largest):
    return jnp.maximum(jnp.ceil(jnp.log2(largest) * FINE), LEAST)


def coded(value, code):
    held = jnp.round(value * (jnp.exp2(code * (-1.0 / FINE)) * FULL))
    return held.astype(jnp.int32).astype(jnp.int16)


def decoded(held, code):
    return held.astype(jnp.float32) * (jnp.exp2(code * (1.0 / FINE)) * (1.0 / FULL))


def codes_of(ref, at):
    return ref[pl.ds(at, SCALE_ROWS), :].astype(jnp.int32).astype(jnp.float32)


def lag_of(offsets_ref, which):
    return offsets_ref[which // LBW] + which % LBW


def fill_rows(turned, at_lane, masked, at_masked, runs, offsets, lag, steps, start_row, chunk):
    actuators = turned.shape[0]
    tiles = chunk // LANES
    lane = lax.broadcasted_iota(jnp.int32, (1, LANES), 1)
    ends, end = [], jnp.int32(0)
    for run in range(runs.shape[0]):
        end = end + runs[run]
        ends.append(end)
    for number, step in enumerate(steps):
        shift = lag_of(offsets, lag ^ step)
        at = at_lane - shift
        base, turn = at // LANES, at % LANES
        low = jnp.broadcast_to(lane < LANES - turn, (actuators, LANES))
        pieces = [
            pltpu.roll(
                turned[:, pl.ds(pl.multiple_of((base + tile) * LANES, LANES), LANES)],
                (LANES - turn) % LANES,
                1,
            )
            for tile in range(tiles + 1)
        ]
        for tile in range(tiles):
            place = lane + (start_row + tile * LANES)
            crossed = jnp.zeros((1, LANES), jnp.int32)
            for end in ends:
                crossed = crossed + ((end <= place) & (end > place - shift)).astype(jnp.int32)
            keep = jnp.broadcast_to(crossed == 0, (actuators, LANES))
            value = jnp.where(low, pieces[tile], pieces[tile + 1])
            value = jnp.where(keep, value, jnp.zeros_like(value))
            masked[pl.ds(number * actuators, actuators), pl.ds(at_masked + tile * LANES, LANES)] = value


def inner_kernel(
    runs_ref, offsets_ref, actuators_ref, sensors_ref, out_ref, first_turned_ref, first_sensed_ref,
    runs, offsets, held, sensed, turned, masked, sems
):
    chunk, lags = LMAX, lax.axis_size("lag")
    samples, _ = actuators_ref.shape
    chunks = samples // chunk
    copies = [
        pltpu.make_async_copy(runs_ref, runs, sems.at[0]),
        pltpu.make_async_copy(offsets_ref, offsets, sems.at[1]),
    ]
    for at in range(chunks):
        here = pl.ds(at * chunk, chunk)
        copies.append(pltpu.make_async_copy(actuators_ref.at[here, :], held.at[here, :], sems.at[2 + at]))
    for at in range(1, chunks):
        copies.append(
            pltpu.make_async_copy(
                sensors_ref.at[pl.ds(at * chunk, chunk), :],
                sensed.at[pl.ds((at - 1) * chunk, chunk), :],
                sems.at[1 + chunks + at],
            )
        )
    copies.append(
        pltpu.make_async_copy(sensors_ref.at[pl.ds(0, chunk), :], first_sensed_ref, sems.at[1 + 2 * chunks])
    )
    for copy in copies:
        copy.start()
    start_row = lax.axis_index("seg") * samples
    for at in range(chunks):
        copies[2 + at].wait()
        here = pl.ds(at * chunk, chunk)
        turned[:, here] = held[here, :].T
        if at == 0:
            first_turned_ref[...] = turned[:, here]
            copies[0].wait()
            copies[1].wait()
            continue
        fill_rows(
            turned, at * chunk, masked, (at - 1) * chunk, runs, offsets,
            lax.axis_index("lag"), range(lags), start_row + at * chunk, chunk,
        )
        copies[1 + chunks + at].wait()
        there = pl.ds((at - 1) * chunk, chunk)
        terms = jnp.dot(masked[:, there], sensed[there, :], preferred_element_type=jnp.float32)
        if at == 1:
            out_ref[...] = terms
        else:
            out_ref[...] += terms
    copies[-1].wait()


def cut_kernel(actuators_ref, out_ref, sem):
    half = out_ref.shape[0]
    start = actuators_ref.shape[0] - LMAX + half * (lax.axis_index("lag") % 2)
    copy = pltpu.make_async_copy(actuators_ref.at[pl.ds(pl.multiple_of(start, 8), half), :], out_ref, sem)
    copy.start()
    copy.wait()


def outer_kernel(
    steps, samples, runs_ref, offsets_ref, mine_ref, theirs_ref, first_turned_ref, sensed_ref, inner_ref,
    near_ref, own_ref, runs, offsets, turned, masked, terms, sems
):
    chunk, segs = LMAX, lax.axis_size("seg")
    far, actuators = segs // 2, inner_ref.shape[0] // lax.axis_size("lag")
    copies = [
        pltpu.make_async_copy(runs_ref, runs, sems.at[0]),
        pltpu.make_async_copy(offsets_ref, offsets, sems.at[1]),
    ]
    for copy in copies:
        copy.start()
    seg, lag = lax.axis_index("seg"), lax.axis_index("lag")
    rows, half = actuators // segs, chunk // 2
    core = lag % 2
    turned[:, pl.ds(pl.multiple_of(core * half, LANES), half)] = mine_ref[...].T
    turned[:, pl.ds(pl.multiple_of((1 - core) * half, LANES), half)] = theirs_ref[...].T
    turned[:, pl.ds(chunk, chunk)] = first_turned_ref[...]
    for copy in copies:
        copy.wait()
    fill_rows(turned, chunk, masked, 0, runs, offsets, lag, steps, seg * samples, chunk)
    for number, step in enumerate(steps):
        here = pl.ds(number * actuators, actuators)
        terms[here, :] = inner_ref[pl.ds(step * actuators, actuators), :]
    terms[...] += jnp.dot(masked[...], sensed_ref[...], preferred_element_type=jnp.float32)

    near_at = seg % 2

    def block_of(number, block, near):
        start = number * actuators + (2 * block + near) * rows
        return terms[pl.ds(pl.multiple_of(start, rows), rows), :]

    codes = []
    for number in range(len(steps)):
        parts = [block_of(number, block, 1 - near_at) for block in range(far)]
        codes.append(put(near_ref, number * far * rows, parts))
        for block in range(far):
            own_ref[pl.ds((number * far + block) * rows, rows), :] = block_of(number, block, near_at)
    put_codes(near_ref, len(steps) * far * rows, codes)


def put(ref, at, parts):
    largest = jnp.abs(parts[0])
    for part in parts[1:]:
        largest = jnp.maximum(largest, jnp.abs(part))
    code = column_code(jnp.max(largest, axis=0, keepdims=True))
    for part in parts:
        ref[pl.ds(at, part.shape[0]), :] = coded(part, code)
        at += part.shape[0]
    return code


def put_codes(ref, at, codes):
    shape = (SCALE_ROWS, codes[0].shape[1])
    sublane = lax.broadcasted_iota(jnp.int32, shape, 0)
    rows = jnp.broadcast_to(codes[0].astype(jnp.int32), shape)
    for row in range(1, len(codes)):
        rows = jnp.where(sublane == row, jnp.broadcast_to(codes[row].astype(jnp.int32), shape), rows)
    ref[pl.ds(at, SCALE_ROWS), :] = rows.astype(jnp.int16)


def second_kernel(count, came_ref, own_ref, total_ref, *far_refs):
    far = lax.axis_size("seg") // 2
    far_refs = (None,) + far_refs
    rows = total_ref.shape[0] // count
    far_at = lax.axis_index("seg") // 2
    codes_came = codes_of(came_ref, count * far * rows)

    def block_sum(number, block):
        here = pl.ds(pl.multiple_of((number * far + block) * rows, rows), rows)
        return own_ref[here, :] + decoded(came_ref[here, :], codes_came[number : number + 1])

    for bits in range(far - 1, 0, -1):
        codes = [
            put(far_refs[bits], number * rows, [block_sum(number, far_at ^ bits)]) for number in range(count)
        ]
        put_codes(far_refs[bits], count * rows, codes)
    for number in range(count):
        total_ref[pl.ds(number * rows, rows), :] = block_sum(number, far_at)


def third_kernel(steps, total_ref, *refs):
    far = lax.axis_size("seg") // 2
    came, outs = refs[: far - 1], refs[far - 1 :]
    rows = total_ref.shape[0] // len(steps)
    codes = [codes_of(ref, len(steps) * rows) for ref in came]
    for number, step in enumerate(steps):
        here = pl.ds(number * rows, rows)
        value = total_ref[here, :]
        for ref, code in zip(came, codes):
            value = value + decoded(ref[here, :], code[number : number + 1])
        if step:
            put_codes(outs[number], rows, [put(outs[number], 0, [value])])
        else:
            outs[number][...] = value


def last_kernel(scaling, own_ref, *refs):
    came, out_ref = (None,) + refs[:-1], refs[-1]
    rows, width = own_ref.shape
    lag = lax.axis_index("lag")
    for step in range(len(came)):
        if step:
            value = decoded(came[step][pl.ds(0, rows), :], codes_of(came[step], rows)[:1])
        else:
            value = own_ref[...]
        out_ref[:, 0, pl.ds(pl.multiple_of((lag ^ step) * width, LANES), width)] = value * scaling


def per_device_staged(actuator_input, sensor_output, run_lengths, lag_offsets):
    samples, actuators = actuator_input.shape
    sensors = sensor_output.shape[1]
    segs, lags = lax.axis_size("seg"), lax.axis_size("lag")
    far, rows, chunk = segs // 2, actuators // segs, LMAX
    scaling = 1.0 / math.sqrt(samples * segs)
    spare = lags * actuators

    def payload(count):
        return jax.ShapeDtypeStruct((count * rows + SCALE_ROWS, sensors), jnp.int16)

    def wide(count):
        return jax.ShapeDtypeStruct((count * rows, sensors), jnp.float32)

    vmem = pl.BlockSpec(memory_space=pltpu.VMEM)
    small = pltpu.CompilerParams(vmem_limit_bytes=8 << 20)
    hbm = pl.BlockSpec(memory_space=pltpu.HBM)
    scalars = [pltpu.SMEM(run_lengths.shape, jnp.int32), pltpu.SMEM(lag_offsets.shape, jnp.int32)]
    chunks = samples // chunk
    run_lengths, lag_offsets, actuator_input, sensor_output = (
        pltpu.with_memory_space_constraint(value, pltpu.HBM)
        for value in (run_lengths, lag_offsets, actuator_input, sensor_output)
    )

    cut = pl.pallas_call(
        cut_kernel,
        in_specs=[hbm],
        out_specs=vmem,
        out_shape=jax.ShapeDtypeStruct((LMAX // 2, actuators), jnp.bfloat16),
        scratch_shapes=[pltpu.SemaphoreType.DMA],
        compiler_params=small,
        name="cut",
    )(actuator_input)
    fetched = shifted_by(cut, "seg", 1)
    swapped = exchange(fetched, 0, 1)

    inner, first_turned, first_sensed = pl.pallas_call(
        inner_kernel,
        in_specs=[hbm] * 4,
        out_specs=[vmem] * 3,
        out_shape=[
            jax.ShapeDtypeStruct((spare, sensors), jnp.float32),
            jax.ShapeDtypeStruct((actuators, chunk), jnp.bfloat16),
            jax.ShapeDtypeStruct((chunk, sensors), jnp.bfloat16),
        ],
        scratch_shapes=scalars
        + [
            pltpu.VMEM((samples, actuators), jnp.bfloat16),
            pltpu.VMEM((samples - chunk, sensors), jnp.bfloat16),
            pltpu.VMEM((actuators, samples + LANES), jnp.bfloat16),
            pltpu.VMEM((spare, samples - chunk), jnp.bfloat16),
            pltpu.SemaphoreType.DMA((2 + 2 * chunks,)),
        ],
        compiler_params=pltpu.CompilerParams(vmem_limit_bytes=40 << 20),
        cost_estimate=pl.CostEstimate(
            flops=2 * spare * sensors * (samples - chunk), bytes_accessed=6 << 20, transcendentals=0
        ),
        name="inner",
    )(run_lengths, lag_offsets, actuator_input, sensor_output)

    def outer(name, steps):
        def body(*refs):
            outer_kernel(steps, samples, *refs)

        return pl.pallas_call(
            body,
            in_specs=[hbm] * 2 + [vmem] * 5,
            out_specs=[vmem] * 2,
            out_shape=[payload(len(steps) * far), wide(len(steps) * far)],
            scratch_shapes=scalars
            + [
                pltpu.VMEM((actuators, 2 * chunk + LANES), jnp.bfloat16),
                pltpu.VMEM((len(steps) * actuators, chunk), jnp.bfloat16),
                pltpu.VMEM((len(steps) * actuators, sensors), jnp.float32),
                pltpu.SemaphoreType.DMA((2,)),
            ],
            compiler_params=pltpu.CompilerParams(vmem_limit_bytes=24 << 20),
            cost_estimate=pl.CostEstimate(
                flops=2 * len(steps) * actuators * sensors * chunk, bytes_accessed=4 << 20, transcendentals=0
            ),
            name=name,
        )(run_lengths, lag_offsets, fetched, swapped, first_turned, first_sensed, inner)

    def second(name, steps, came, own):
        def body(*refs):
            second_kernel(len(steps), *refs)

        return pl.pallas_call(
            body,
            in_specs=[vmem] * 2,
            out_specs=[vmem] * far,
            out_shape=[wide(len(steps))] + [payload(len(steps))] * (far - 1),
            compiler_params=small,
            cost_estimate=pl.CostEstimate(flops=1 << 20, bytes_accessed=2 << 20, transcendentals=0),
            name=name,
        )(came, own)

    def third(name, steps, total, *came):
        def body(*refs):
            third_kernel(steps, *refs)

        return pl.pallas_call(
            body,
            in_specs=[vmem] * far,
            out_specs=[vmem] * len(steps),
            out_shape=[payload(1) if step else wide(1) for step in steps],
            compiler_params=small,
            cost_estimate=pl.CostEstimate(flops=1 << 20, bytes_accessed=1 << 20, transcendentals=0),
            name=name,
        )(total, *came)

    masks = range(far - 1, 0, -1)
    groups = (tuple(range(lags - 1, lags // 2 - 1, -1)), tuple(range(lags // 2 - 1, -1, -1)))
    names = ("a", "b")
    near, kept, total, ended = {}, {}, {}, {}
    for name, steps in zip(names, groups):
        send, kept[name] = outer("outer_" + name, steps)
        near[name] = exchange(send, 1, 0)
    for name, steps in zip(names, groups):
        total[name], *sends = second("second_" + name, steps, near[name], kept[name])
        near[name] = [exchange(sends[bits - 1], 2 * bits, 0) for bits in masks][::-1]
    for name, steps in zip(names, groups):
        outs = third("third_" + name, steps, total[name], *near[name])
        for step, out in zip(steps, outs):
            ended[step] = exchange(out, 0, step) if step else out

    def last_body(*refs):
        return last_kernel(scaling, *refs)

    return pl.pallas_call(
        last_body,
        in_specs=[vmem] * lags,
        out_specs=vmem,
        out_shape=jax.ShapeDtypeStruct((rows, 1, lags * sensors), jnp.float32),
        compiler_params=small,
        name="last",
    )(*[ended[step] for step in range(lags)])


def solution(mesh):
    segs, lags = mesh.shape["seg"], mesh.shape["lag"]

    def per_device(actuator_input, sensor_output, run_lengths, lag_offsets):
        rows = actuator_input.shape[1] // segs
        staged = (
            4 <= segs <= 16
            and segs & (segs - 1) == 0
            and lags & (lags - 1) == 0
            and lags == NBLK * LBW
            and rows % 8 == 0
            and actuator_input.shape[0] % LMAX == 0
            and actuator_input.shape[0] > LMAX
        )
        chosen = per_device_staged if staged else per_device_plain
        return chosen(actuator_input, sensor_output, run_lengths, lag_offsets)

    mapped = jax.shard_map(
        per_device,
        mesh=mesh,
        in_specs=(P("seg", None), P("seg", "lag"), P(), P()),
        out_specs=P("seg", "lag", None),
        check_vma=False,
    )
    return mapped
    return mapped
    return mapped
    return mapped
    return mapped
    return mapped
```

```python
import math

import jax
import jax.numpy as jnp
from jax import lax
from jax.experimental import pallas as pl
from jax.experimental.pallas import tpu as pltpu
from jax.experimental import pallas as pl
from jax.experimental.pallas import tpu as pltpu
from jax.experimental import pallas as pl
from jax.experimental.pallas import tpu as pltpu
from jax.experimental import pallas as pl
from jax.experimental.pallas import tpu as pltpu
from jax.experimental import pallas as pl
from jax.experimental.pallas import tpu as pltpu
from jax.experimental import pallas as pl
from jax.experimental.pallas import tpu as pltpu
from jax.experimental import pallas as pl
from jax.experimental.pallas import tpu as pltpu
from jax.sharding import PartitionSpec as P


LMAX = 1024
LBW = 2
NBLK = 2
FINE = 64.0
FULL = 32700.0
LEAST = -112.0 * FINE
SCALE_ROWS = 8
LANES = 128
LANES = 128
LANES = 128
LANES = 128
LANES = 128
LANES = 128
LANES = 128


def shifted_by(value, axis, steps):
    count = lax.axis_size(axis)
    initial, last = (max(0, -steps), min(count, count - steps))
    return lax.ppermute(value, axis, [(source, source + steps) for source in range(initial, last)])


def segment_ids(run_lengths, start_row, row_count):
    run_ends = jnp.cumsum(run_lengths)
    places = start_row + jnp.arange(row_count, dtype=jnp.int32)
    return jnp.sum((run_ends[None, :] <= places[:, None]).astype(jnp.int32), axis=1)


def product_over_time(masked, shifted):
    return lax.dot_general(
        masked, shifted, (((0,), (0,)), ((), ())), preferred_element_type=jnp.float32
    )


def per_device_plain(actuator_input, sensor_output, run_lengths, lag_offsets):
    samples = actuator_input.shape[0]
    devices_seg = lax.axis_size("seg")
    scaling = 1.0 / math.sqrt(samples * devices_seg)
    start_row = lax.axis_index("seg") * samples
    halo_rows = shifted_by(sensor_output[:LMAX], "seg", -1)
    idents = segment_ids(run_lengths, start_row, samples + LMAX)
    own_ids = idents[:samples]
    shifts = [lag_offsets[blk_num] + lag_step for blk_num in range(NBLK) for lag_step in range(LBW)]
    joined = jnp.concatenate([sensor_output, halo_rows], axis=0)

    def lag_term(lag_value):
        shifted = lax.dynamic_slice_in_dim(joined, lag_value, samples, 0)
        shifted_ids = lax.dynamic_slice_in_dim(idents, lag_value, samples, 0)
        masked = jnp.where((own_ids == shifted_ids)[:, None], actuator_input, jnp.zeros_like(actuator_input))
        return product_over_time(masked, shifted)

    shares = lax.psum_scatter(
        jnp.stack([lag_term(lag_value) for lag_value in shifts], axis=1),
        "seg",
        scatter_dimension=0,
        tiled=True,
    )
    result_rows = lax.all_to_all(shares, "lag", split_axis=1, concat_axis=2, tiled=True)
    return result_rows * scaling


def exchange(value, seg_bits, lag_bits):
    segs, lags = lax.axis_size("seg"), lax.axis_size("lag")
    pairs = [
        (s * lags + l, (s ^ seg_bits) * lags + (l ^ lag_bits)) for s in range(segs) for l in range(lags)
    ]
    return lax.ppermute(value, ("seg", "lag"), pairs)


def column_code(largest):
    return jnp.maximum(jnp.ceil(jnp.log2(largest) * FINE), LEAST)


def scale_rows(count, width):
    return -(-count * (width // LANES) // SCALE_ROWS) * SCALE_ROWS


def put(ref, at, parts, stride):
    largest = jnp.abs(parts[0])
    for part in parts[1:]:
        largest = jnp.maximum(largest, jnp.abs(part))
    code = column_code(jnp.max(largest, axis=0, keepdims=True))
    factor = jnp.exp2(code * (-1.0 / FINE)) * FULL
    rows, width = parts[0].shape
    for number, part in enumerate(parts):
        held = jnp.round(part * factor).astype(jnp.int32).astype(jnp.int16)
        for lanes in range(width // LANES):
            ref[pl.ds(at + number * stride + lanes * rows, rows), :] = held[:, lanes * LANES : (lanes + 1) * LANES]
    return code


def put_codes(ref, at, codes):
    width = codes[0].shape[1]
    pieces = [code[:, start : start + LANES] for code in codes for start in range(0, width, LANES)]
    count = scale_rows(len(codes), width)
    shape = (count, LANES)
    sublane = lax.broadcasted_iota(jnp.int32, shape, 0)
    rows = jnp.broadcast_to(pieces[0].astype(jnp.int32), shape)
    for row in range(1, len(pieces)):
        rows = jnp.where(sublane == row, jnp.broadcast_to(pieces[row].astype(jnp.int32), shape), rows)
    ref[pl.ds(at, count), :] = rows.astype(jnp.int16)


def scales_of(ref, at, count, width):
    codes = ref[pl.ds(at, scale_rows(count, width)), :].astype(jnp.int32).astype(jnp.float32)
    return jnp.exp2(codes * (1.0 / FINE)) * (1.0 / FULL)


def opened(ref, at, scales, number, rows, width):
    lanes = width // LANES
    return jnp.concatenate(
        [
            ref[pl.ds(at + block * rows, rows), :].astype(jnp.float32)
            * scales[number * lanes + block : number * lanes + block + 1]
            for block in range(lanes)
        ],
        axis=1,
    )


def lag_of(offsets_ref, which):
    return offsets_ref[which // LBW] + which % LBW


def fill_rows(turned, at_lane, masked, at_masked, runs, offsets, lag, steps, start_row, chunk):
    actuators = turned.shape[0]
    tiles = chunk // LANES
    lane = lax.broadcasted_iota(jnp.int32, (1, LANES), 1)
    ends, end = [], jnp.int32(0)
    for run in range(runs.shape[0]):
        end = end + runs[run]
        ends.append(end)
    for number, step in enumerate(steps):
        shift = lag_of(offsets, lag ^ step)
        at = at_lane - shift
        base, turn = at // LANES, at % LANES
        low = jnp.broadcast_to(lane < LANES - turn, (actuators, LANES))
        pieces = [
            pltpu.roll(
                turned[:, pl.ds(pl.multiple_of((base + tile) * LANES, LANES), LANES)],
                (LANES - turn) % LANES,
                1,
            )
            for tile in range(tiles + 1)
        ]
        for tile in range(tiles):
            place = lane + (start_row + tile * LANES)
            crossed = jnp.zeros((1, LANES), jnp.int32)
            for end in ends:
                crossed = crossed + ((end <= place) & (end > place - shift)).astype(jnp.int32)
            keep = jnp.broadcast_to(crossed == 0, (actuators, LANES))
            value = jnp.where(low, pieces[tile], pieces[tile + 1])
            value = jnp.where(keep, value, jnp.zeros_like(value))
            masked[pl.ds(number * actuators, actuators), pl.ds(at_masked + tile * LANES, LANES)] = value


def inner_kernel(
    runs_ref, offsets_ref, actuators_ref, sensors_ref, out_ref, first_turned_ref, first_sensed_ref,
    runs, offsets, held, sensed, turned, masked, sems
):
    chunk, lags = LMAX, lax.axis_size("lag")
    samples, _ = actuators_ref.shape
    chunks = samples // chunk
    copies = [
        pltpu.make_async_copy(runs_ref, runs, sems.at[0]),
        pltpu.make_async_copy(offsets_ref, offsets, sems.at[1]),
    ]
    for at in range(chunks):
        here = pl.ds(at * chunk, chunk)
        copies.append(pltpu.make_async_copy(actuators_ref.at[here, :], held.at[here, :], sems.at[2 + at]))
    for at in range(1, chunks):
        copies.append(
            pltpu.make_async_copy(
                sensors_ref.at[pl.ds(at * chunk, chunk), :],
                sensed.at[pl.ds((at - 1) * chunk, chunk), :],
                sems.at[1 + chunks + at],
            )
        )
    copies.append(
        pltpu.make_async_copy(sensors_ref.at[pl.ds(0, chunk), :], first_sensed_ref, sems.at[1 + 2 * chunks])
    )
    for copy in copies:
        copy.start()
    start_row = lax.axis_index("seg") * samples
    for at in range(chunks):
        copies[2 + at].wait()
        here = pl.ds(at * chunk, chunk)
        turned[:, here] = held[here, :].T
        if at == 0:
            first_turned_ref[...] = turned[:, here]
            copies[0].wait()
            copies[1].wait()
            continue
        fill_rows(
            turned, at * chunk, masked, (at - 1) * chunk, runs, offsets,
            lax.axis_index("lag"), range(lags), start_row + at * chunk, chunk,
        )
        copies[1 + chunks + at].wait()
        there = pl.ds((at - 1) * chunk, chunk)
        terms = jnp.dot(masked[:, there], sensed[there, :], preferred_element_type=jnp.float32)
        if at == 1:
            out_ref[...] = terms
        else:
            out_ref[...] += terms
    copies[-1].wait()


def cut_kernel(actuators_ref, out_ref, sem):
    half = out_ref.shape[0]
    start = actuators_ref.shape[0] - LMAX + half * (lax.axis_index("lag") % 2)
    copy = pltpu.make_async_copy(actuators_ref.at[pl.ds(pl.multiple_of(start, 8), half), :], out_ref, sem)
    copy.start()
    copy.wait()


def outer_terms(
    steps, samples, runs_ref, offsets_ref, mine_ref, theirs_ref, first_turned_ref, sensed_ref, inner_ref,
    runs, offsets, turned, masked, terms, sems
):
    chunk, segs = LMAX, lax.axis_size("seg")
    actuators = inner_ref.shape[0] // lax.axis_size("lag")
    copies = [
        pltpu.make_async_copy(runs_ref, runs, sems.at[0]),
        pltpu.make_async_copy(offsets_ref, offsets, sems.at[1]),
    ]
    for copy in copies:
        copy.start()
    seg, lag = lax.axis_index("seg"), lax.axis_index("lag")
    rows, half = actuators // segs, chunk // 2
    core = lag % 2
    turned[:, pl.ds(pl.multiple_of(core * half, LANES), half)] = mine_ref[...].T
    turned[:, pl.ds(pl.multiple_of((1 - core) * half, LANES), half)] = theirs_ref[...].T
    turned[:, pl.ds(chunk, chunk)] = first_turned_ref[...]
    for copy in copies:
        copy.wait()
    fill_rows(turned, chunk, masked, 0, runs, offsets, lag, steps, seg * samples, chunk)
    for number, step in enumerate(steps):
        here = pl.ds(number * actuators, actuators)
        terms[here, :] = inner_ref[pl.ds(step * actuators, actuators), :]
    terms[...] += jnp.dot(masked[...], sensed_ref[...], preferred_element_type=jnp.float32)

    def block_of(number, block, near):
        start = number * actuators + (2 * block + near) * rows
        return terms[pl.ds(pl.multiple_of(start, rows), rows), :]

    return block_of, rows, rows * (inner_ref.shape[1] // LANES)


def outer_group_kernel(steps, samples, *refs):
    far, inputs = lax.axis_size("seg") // 2, refs[:7]
    send_ref, own_ref = refs[7:9]
    block_of, rows, size = outer_terms(steps, samples, *inputs, *refs[-6:])
    near_at = lax.axis_index("seg") % 2
    codes = []
    for number in range(len(steps)):
        parts = [block_of(number, block, 1 - near_at) for block in range(far)]
        codes.append(put(send_ref, number * far * size, parts, size))
        for block in range(far):
            own_ref[pl.ds((number * far + block) * rows, rows), :] = block_of(number, block, near_at)
    put_codes(send_ref, len(steps) * far * size, codes)


def outer_near_kernel(samples, *refs):
    far, inputs = lax.axis_size("seg") // 2, refs[:7]
    send_one_ref, send_own_ref, kept_one_ref, own_ref = refs[7:11]
    block_of, rows, size = outer_terms((1, 0), samples, *inputs, *refs[-6:])
    near_at = lax.axis_index("seg") % 2

    def send(ref, number, near):
        parts = [block_of(number, block, near) for block in range(far)]
        put_codes(ref, far * size, [put(ref, 0, parts, size)])

    send(send_one_ref, 0, 1 - near_at)
    send(send_own_ref, 1, 1 - near_at)
    send(kept_one_ref, 0, near_at)
    for block in range(far):
        own_ref[pl.ds(block * rows, rows), :] = block_of(1, block, near_at)


def second_near_kernel(came_one_ref, came_own_ref, kept_one_ref, own_ref, total_ref, *far_refs):
    far = lax.axis_size("seg") // 2
    far_refs = (None,) + far_refs
    rows, sensors = total_ref.shape[0] // 2, total_ref.shape[1]
    size = rows * (sensors // LANES)
    far_at = lax.axis_index("seg") // 2
    one, own, kept = (
        scales_of(ref, far * size, 1, sensors) for ref in (came_one_ref, came_own_ref, kept_one_ref)
    )

    def block_sum(step, block):
        at = pl.multiple_of(block * size, rows)
        if step:
            return opened(came_one_ref, at, one, 0, rows, sensors) + opened(kept_one_ref, at, kept, 0, rows, sensors)
        mine = own_ref[pl.ds(pl.multiple_of(block * rows, rows), rows), :]
        return mine + opened(came_own_ref, at, own, 0, rows, sensors)

    for bits in range(far - 1, 0, -1):
        codes = [put(far_refs[bits], step * size, [block_sum(step, far_at ^ bits)], size) for step in range(2)]
        put_codes(far_refs[bits], 2 * size, codes)
    for step in range(2):
        total_ref[pl.ds(step * rows, rows), :] = block_sum(step, far_at)


def far_sum(start, came, scales, number, rows, sensors):
    value = start
    size = rows * (sensors // LANES)
    for ref, scale in zip(came, scales):
        value = value + opened(ref, pl.multiple_of(number * size, rows), scale, number, rows, sensors)
    return value


def second_kernel(count, came_ref, own_ref, total_ref, *far_refs):
    far = lax.axis_size("seg") // 2
    far_refs = (None,) + far_refs
    rows, sensors = total_ref.shape[0] // count, total_ref.shape[1]
    size = rows * (sensors // LANES)
    far_at = lax.axis_index("seg") // 2
    scales = scales_of(came_ref, count * far * size, count, sensors)

    def block_sum(number, block):
        at = number * far + block
        return own_ref[pl.ds(pl.multiple_of(at * rows, rows), rows), :] + opened(
            came_ref, pl.multiple_of(at * size, rows), scales, number, rows, sensors
        )

    for bits in range(far - 1, 0, -1):
        codes = [put(far_refs[bits], number * size, [block_sum(number, far_at ^ bits)], size) for number in range(count)]
        put_codes(far_refs[bits], count * size, codes)
    for number in range(count):
        total_ref[pl.ds(number * rows, rows), :] = block_sum(number, far_at)


def third_kernel(count, total_ref, *refs):
    came, outs = refs[:-count], refs[-count:]
    rows, sensors = total_ref.shape[0] // count, total_ref.shape[1]
    size = rows * (sensors // LANES)
    scales = [scales_of(ref, count * size, count, sensors) for ref in came]
    for number in range(count):
        value = far_sum(total_ref[pl.ds(number * rows, rows), :], came, scales, number, rows, sensors)
        put_codes(outs[number], size, [put(outs[number], 0, [value], size)])


def last_kernel(scaling, steps, total_ref, *refs):
    far, out_ref = lax.axis_size("seg") // 2, refs[-1]
    came_far, came = refs[: far - 1], refs[far - 1 : -1]
    rows, sensors = total_ref.shape[0] // 2, total_ref.shape[1]
    size = rows * (sensors // LANES)
    lag = lax.axis_index("lag")

    def write(step, value):
        out_ref[:, 0, pl.ds(pl.multiple_of((lag ^ step) * sensors, LANES), sensors)] = value * scaling

    for number, step in enumerate(steps):
        write(step, opened(came[number], 0, scales_of(came[number], size, 1, sensors), 0, rows, sensors))
    scales = [scales_of(ref, 2 * size, 2, sensors) for ref in came_far]
    for step in range(2):
        write(step, far_sum(total_ref[pl.ds(step * rows, rows), :], came_far, scales, step, rows, sensors))


def per_device_staged(actuator_input, sensor_output, run_lengths, lag_offsets):
    samples, actuators = actuator_input.shape
    sensors = sensor_output.shape[1]
    segs, lags = lax.axis_size("seg"), lax.axis_size("lag")
    far, rows, chunk = segs // 2, actuators // segs, LMAX
    scaling = 1.0 / math.sqrt(samples * segs)
    spare = lags * actuators

    def payload(count, codes):
        return jax.ShapeDtypeStruct(
            (count * rows * (sensors // LANES) + scale_rows(codes, sensors), LANES), jnp.int16
        )

    def wide(count):
        return jax.ShapeDtypeStruct((count * rows, sensors), jnp.float32)

    vmem = pl.BlockSpec(memory_space=pltpu.VMEM)
    small = pltpu.CompilerParams(vmem_limit_bytes=8 << 20)
    hbm = pl.BlockSpec(memory_space=pltpu.HBM)
    scalars = [pltpu.SMEM(run_lengths.shape, jnp.int32), pltpu.SMEM(lag_offsets.shape, jnp.int32)]
    chunks = samples // chunk
    run_lengths, lag_offsets, actuator_input, sensor_output = (
        pltpu.with_memory_space_constraint(value, pltpu.HBM)
        for value in (run_lengths, lag_offsets, actuator_input, sensor_output)
    )

    cut = pl.pallas_call(
        cut_kernel,
        in_specs=[hbm],
        out_specs=vmem,
        out_shape=jax.ShapeDtypeStruct((LMAX // 2, actuators), jnp.bfloat16),
        scratch_shapes=[pltpu.SemaphoreType.DMA],
        compiler_params=small,
        name="cut",
    )(actuator_input)
    fetched = shifted_by(cut, "seg", 1)
    swapped = exchange(fetched, 0, 1)

    inner, first_turned, first_sensed = pl.pallas_call(
        inner_kernel,
        in_specs=[hbm] * 4,
        out_specs=[vmem] * 3,
        out_shape=[
            jax.ShapeDtypeStruct((spare, sensors), jnp.float32),
            jax.ShapeDtypeStruct((actuators, chunk), jnp.bfloat16),
            jax.ShapeDtypeStruct((chunk, sensors), jnp.bfloat16),
        ],
        scratch_shapes=scalars
        + [
            pltpu.VMEM((samples, actuators), jnp.bfloat16),
            pltpu.VMEM((samples - chunk, sensors), jnp.bfloat16),
            pltpu.VMEM((actuators, samples + LANES), jnp.bfloat16),
            pltpu.VMEM((spare, samples - chunk), jnp.bfloat16),
            pltpu.SemaphoreType.DMA((2 + 2 * chunks,)),
        ],
        compiler_params=pltpu.CompilerParams(vmem_limit_bytes=40 << 20),
        cost_estimate=pl.CostEstimate(
            flops=2 * spare * sensors * (samples - chunk), bytes_accessed=6 << 20, transcendentals=0
        ),
        name="inner",
    )(run_lengths, lag_offsets, actuator_input, sensor_output)

    def outer(name, body, count, shapes):
        return pl.pallas_call(
            body,
            in_specs=[hbm] * 2 + [vmem] * 5,
            out_specs=[vmem] * len(shapes),
            out_shape=shapes,
            scratch_shapes=scalars
            + [
                pltpu.VMEM((actuators, 2 * chunk + LANES), jnp.bfloat16),
                pltpu.VMEM((count * actuators, chunk), jnp.bfloat16),
                pltpu.VMEM((count * actuators, sensors), jnp.float32),
                pltpu.SemaphoreType.DMA((2,)),
            ],
            compiler_params=pltpu.CompilerParams(vmem_limit_bytes=24 << 20),
            cost_estimate=pl.CostEstimate(
                flops=2 * count * actuators * sensors * chunk, bytes_accessed=4 << 20, transcendentals=0
            ),
            name=name,
        )(run_lengths, lag_offsets, fetched, swapped, first_turned, first_sensed, inner)

    def local(name, body, shapes, *operands):
        return pl.pallas_call(
            body,
            in_specs=[vmem] * len(operands),
            out_specs=[vmem] * len(shapes),
            out_shape=shapes,
            compiler_params=small,
            cost_estimate=pl.CostEstimate(flops=1 << 20, bytes_accessed=1 << 20, transcendentals=0),
            name=name,
        )(*operands)

    def far_exchange(sends):
        came = [None] * (far - 1)
        for bits in range(far - 1, 0, -1):
            came[bits - 1] = exchange(sends[bits - 1], 2 * bits, 0)
        return came

    steps = tuple(range(lags - 1, 1, -1))
    count = len(steps)

    def outer_a(*refs):
        outer_group_kernel(steps, samples, *refs)

    def outer_b(*refs):
        outer_near_kernel(samples, *refs)

    def second_a(*refs):
        second_kernel(count, *refs)

    def third_a(*refs):
        third_kernel(count, *refs)

    def last_body(*refs):
        last_kernel(scaling, steps, *refs)

    send_a, own_a = outer("outer_a", outer_a, count, [payload(count * far, count), wide(count * far)])
    came_a = exchange(send_a, 1, 0)
    send_one, send_own, kept_one, own_b = outer("outer_b", outer_b, 2, [payload(far, 1)] * 3 + [wide(far)])
    came_one = exchange(send_one, 1, 1)
    came_own = exchange(send_own, 1, 0)
    kept_one = exchange(kept_one, 0, 1)
    total_a, *sends_a = local("second_a", second_a, [wide(count)] + [payload(count, count)] * (far - 1), came_a, own_a)
    far_a = far_exchange(sends_a)
    total_b, *sends_b = local(
        "second_b",
        second_near_kernel,
        [wide(2)] + [payload(2, 2)] * (far - 1),
        came_one,
        came_own,
        kept_one,
        own_b,
    )
    far_b = far_exchange(sends_b)
    outs = local("third_a", third_a, [payload(1, 1)] * count, total_a, *far_a)
    came = [exchange(out, 0, step) for step, out in zip(steps, outs)]
    return local(
        "last",
        last_body,
        [jax.ShapeDtypeStruct((rows, 1, lags * sensors), jnp.float32)],
        total_b,
        *far_b,
        *came,
    )[0]


def solution(mesh):
    segs, lags = mesh.shape["seg"], mesh.shape["lag"]

    def per_device(actuator_input, sensor_output, run_lengths, lag_offsets):
        rows, sensors = actuator_input.shape[1] // segs, sensor_output.shape[1]
        staged = (
            4 <= segs <= 16
            and segs & (segs - 1) == 0
            and lags & (lags - 1) == 0
            and lags == NBLK * LBW
            and lags >= 4
            and rows % 8 == 0
            and sensors % LANES == 0
            and actuator_input.shape[0] % LMAX == 0
            and actuator_input.shape[0] > LMAX
        )
        chosen = per_device_staged if staged else per_device_plain
        return chosen(actuator_input, sensor_output, run_lengths, lag_offsets)

    return jax.shard_map(
        per_device,
        mesh=mesh,
        in_specs=(P("seg", None), P("seg", "lag"), P(), P()),
        out_specs=P("seg", "lag", None),
        check_vma=False,
    )
```

```python
import math

import jax
import jax.numpy as jnp
from jax import lax
from jax.experimental import pallas as pl
from jax.experimental.pallas import tpu as pltpu
from jax.experimental import pallas as pl
from jax.experimental.pallas import tpu as pltpu
from jax.experimental import pallas as pl
from jax.experimental.pallas import tpu as pltpu
from jax.experimental import pallas as pl
from jax.experimental.pallas import tpu as pltpu
from jax.experimental import pallas as pl
from jax.experimental.pallas import tpu as pltpu
from jax.experimental import pallas as pl
from jax.experimental.pallas import tpu as pltpu
from jax.experimental import pallas as pl
from jax.experimental.pallas import tpu as pltpu
from jax.sharding import PartitionSpec as P


LMAX = 1024
LBW = 2
NBLK = 2
FINE = 64.0
FULL = 32700.0
LEAST = -112.0 * FINE
SCALE_ROWS = 8
LANES = 128
LANES = 128
LANES = 128
LANES = 128
LANES = 128
LANES = 128
LANES = 128


def shifted_by(value, axis, steps):
    count = lax.axis_size(axis)
    initial, last = (max(0, -steps), min(count, count - steps))
    return lax.ppermute(value, axis, [(source, source + steps) for source in range(initial, last)])


def segment_ids(run_lengths, start_row, row_count):
    run_ends = jnp.cumsum(run_lengths)
    places = start_row + jnp.arange(row_count, dtype=jnp.int32)
    return jnp.sum((run_ends[None, :] <= places[:, None]).astype(jnp.int32), axis=1)


def product_over_time(masked, shifted):
    return lax.dot_general(
        masked, shifted, (((0,), (0,)), ((), ())), preferred_element_type=jnp.float32
    )


def per_device_plain(actuator_input, sensor_output, run_lengths, lag_offsets):
    samples = actuator_input.shape[0]
    devices_seg = lax.axis_size("seg")
    scaling = 1.0 / math.sqrt(samples * devices_seg)
    start_row = lax.axis_index("seg") * samples
    halo_rows = shifted_by(sensor_output[:LMAX], "seg", -1)
    idents = segment_ids(run_lengths, start_row, samples + LMAX)
    own_ids = idents[:samples]
    shifts = [lag_offsets[blk_num] + lag_step for blk_num in range(NBLK) for lag_step in range(LBW)]
    joined = jnp.concatenate([sensor_output, halo_rows], axis=0)

    def lag_term(lag_value):
        shifted = lax.dynamic_slice_in_dim(joined, lag_value, samples, 0)
        shifted_ids = lax.dynamic_slice_in_dim(idents, lag_value, samples, 0)
        masked = jnp.where((own_ids == shifted_ids)[:, None], actuator_input, jnp.zeros_like(actuator_input))
        return product_over_time(masked, shifted)

    shares = lax.psum_scatter(
        jnp.stack([lag_term(lag_value) for lag_value in shifts], axis=1),
        "seg",
        scatter_dimension=0,
        tiled=True,
    )
    result_rows = lax.all_to_all(shares, "lag", split_axis=1, concat_axis=2, tiled=True)
    return result_rows * scaling


def exchange(value, seg_bits, lag_bits):
    segs, lags = lax.axis_size("seg"), lax.axis_size("lag")
    pairs = [
        (s * lags + l, (s ^ seg_bits) * lags + (l ^ lag_bits)) for s in range(segs) for l in range(lags)
    ]
    return lax.ppermute(value, ("seg", "lag"), pairs)


def column_code(largest):
    return jnp.maximum(jnp.ceil(jnp.log2(largest) * FINE), LEAST)


def scale_rows(count, width):
    return -(-count * (width // LANES) // SCALE_ROWS) * SCALE_ROWS


def put(ref, at, parts, stride):
    largest = jnp.abs(parts[0])
    for part in parts[1:]:
        largest = jnp.maximum(largest, jnp.abs(part))
    code = column_code(jnp.max(largest, axis=0, keepdims=True))
    factor = jnp.exp2(code * (-1.0 / FINE)) * FULL
    rows, width = parts[0].shape
    for number, part in enumerate(parts):
        held = jnp.round(part * factor).astype(jnp.int32).astype(jnp.int16)
        for lanes in range(width // LANES):
            ref[pl.ds(at + number * stride + lanes * rows, rows), :] = held[:, lanes * LANES : (lanes + 1) * LANES]
    return code


def put_codes(ref, at, codes):
    width = codes[0].shape[1]
    pieces = [code[:, start : start + LANES] for code in codes for start in range(0, width, LANES)]
    count = scale_rows(len(codes), width)
    shape = (count, LANES)
    sublane = lax.broadcasted_iota(jnp.int32, shape, 0)
    rows = jnp.broadcast_to(pieces[0].astype(jnp.int32), shape)
    for row in range(1, len(pieces)):
        rows = jnp.where(sublane == row, jnp.broadcast_to(pieces[row].astype(jnp.int32), shape), rows)
    ref[pl.ds(at, count), :] = rows.astype(jnp.int16)


def scales_of(ref, at, count, width):
    codes = ref[pl.ds(at, scale_rows(count, width)), :].astype(jnp.int32).astype(jnp.float32)
    return jnp.exp2(codes * (1.0 / FINE)) * (1.0 / FULL)


def opened(ref, at, scales, number, rows, width):
    lanes = width // LANES
    return jnp.concatenate(
        [
            ref[pl.ds(at + block * rows, rows), :].astype(jnp.float32)
            * scales[number * lanes + block : number * lanes + block + 1]
            for block in range(lanes)
        ],
        axis=1,
    )


def lag_of(offsets_ref, which):
    return offsets_ref[which // LBW] + which % LBW


def put_turned(turned, at_lane, value):
    segs = lax.axis_size("seg")
    actuators = value.shape[1]
    rows, near_at = actuators // segs, lax.axis_index("seg") % 2
    across = value.T
    for at in range(segs):
        mine = (near_at + at + 1) % 2
        start = mine * (actuators // 2) + (at // 2) * rows
        turned[pl.ds(pl.multiple_of(start, rows), rows), pl.ds(at_lane, value.shape[0])] = across[
            at * rows : (at + 1) * rows
        ]


def fill_rows(turned, at_lane, masked, at_masked, runs, offsets, lag, blocks, start_row, chunk):
    tiles = chunk // LANES
    lane = lax.broadcasted_iota(jnp.int32, (1, LANES), 1)
    ends, end = [], jnp.int32(0)
    for run in range(runs.shape[0]):
        end = end + runs[run]
        ends.append(end)
    at_row = 0
    for step, first_row, actuators in blocks:
        shift = lag_of(offsets, lag ^ step)
        at = at_lane - shift
        base, turn = at // LANES, at % LANES
        low = jnp.broadcast_to(lane < LANES - turn, (actuators, LANES))
        pieces = [
            pltpu.roll(
                turned[
                    pl.ds(first_row, actuators), pl.ds(pl.multiple_of((base + tile) * LANES, LANES), LANES)
                ],
                (LANES - turn) % LANES,
                1,
            )
            for tile in range(tiles + 1)
        ]
        for tile in range(tiles):
            place = lane + (start_row + tile * LANES)
            crossed = jnp.zeros((1, LANES), jnp.int32)
            for end in ends:
                crossed = crossed + ((end <= place) & (end > place - shift)).astype(jnp.int32)
            keep = jnp.broadcast_to(crossed == 0, (actuators, LANES))
            value = jnp.where(low, pieces[tile], pieces[tile + 1])
            value = jnp.where(keep, value, jnp.zeros_like(value))
            masked[pl.ds(at_row, actuators), pl.ds(at_masked + tile * LANES, LANES)] = value
        at_row += actuators


def inner_kernel(
    runs_ref, offsets_ref, actuators_ref, sensors_ref, out_ref, first_turned_ref, first_sensed_ref,
    runs_out, offsets_out, runs, offsets, held, sensed, turned, masked, sems
):
    chunk, lags = LMAX, lax.axis_size("lag")
    samples, actuators = actuators_ref.shape
    chunks = samples // chunk
    copies = [
        pltpu.make_async_copy(runs_ref, runs, sems.at[0]),
        pltpu.make_async_copy(offsets_ref, offsets, sems.at[1]),
    ]
    for at in range(chunks):
        here = pl.ds(at * chunk, chunk)
        copies.append(pltpu.make_async_copy(actuators_ref.at[here, :], held.at[here, :], sems.at[2 + at]))
    for at in range(1, chunks):
        copies.append(
            pltpu.make_async_copy(
                sensors_ref.at[pl.ds(at * chunk, chunk), :],
                sensed.at[pl.ds((at - 1) * chunk, chunk), :],
                sems.at[1 + chunks + at],
            )
        )
    copies.append(
        pltpu.make_async_copy(sensors_ref.at[pl.ds(0, chunk), :], first_sensed_ref, sems.at[1 + 2 * chunks])
    )
    copies.append(pltpu.make_async_copy(runs_ref, runs_out, sems.at[2 + 2 * chunks]))
    copies.append(pltpu.make_async_copy(offsets_ref, offsets_out, sems.at[3 + 2 * chunks]))
    for copy in copies:
        copy.start()
    start_row = lax.axis_index("seg") * samples
    for at in range(chunks):
        copies[2 + at].wait()
        here = pl.ds(at * chunk, chunk)
        put_turned(turned, at * chunk, held[here, :])
        if at == 0:
            first_turned_ref[:, pl.ds(chunk, chunk)] = turned[:, here]
            copies[0].wait()
            copies[1].wait()
            continue
        fill_rows(
            turned, at * chunk, masked, (at - 1) * chunk, runs, offsets,
            lax.axis_index("lag"), [(step, 0, actuators) for step in range(lags)], start_row + at * chunk, chunk,
        )
        copies[1 + chunks + at].wait()
        there = pl.ds((at - 1) * chunk, chunk)
        terms = jnp.dot(masked[:, there], sensed[there, :], preferred_element_type=jnp.float32)
        if at == 1:
            out_ref[...] = terms
        else:
            out_ref[...] += terms
    for copy in copies[-3:]:
        copy.wait()


def cut_kernel(actuators_ref, out_ref, sem):
    half = out_ref.shape[0]
    start = actuators_ref.shape[0] - LMAX + half * (lax.axis_index("lag") % 2)
    copy = pltpu.make_async_copy(actuators_ref.at[pl.ds(pl.multiple_of(start, 8), half), :], out_ref, sem)
    copy.start()
    copy.wait()


def outer_terms(
    blocks, samples, runs_ref, offsets_ref, turned, sensed_ref, inner_ref, runs, offsets, masked, terms, sems, tails=()
):
    chunk = LMAX
    copies = [
        pltpu.make_async_copy(runs_ref, runs, sems.at[0]),
        pltpu.make_async_copy(offsets_ref, offsets, sems.at[1]),
    ]
    for copy in copies:
        copy.start()
    actuators = inner_ref.shape[0] // lax.axis_size("lag")
    lag, half = lax.axis_index("lag"), chunk // 2
    for number, tail_ref in enumerate(tails):
        place = (lag + number) % 2
        put_turned(turned, pl.multiple_of(place * half, LANES), tail_ref[...])
    for copy in copies:
        copy.wait()
    fill_rows(turned, chunk, masked, 0, runs, offsets, lag, blocks, lax.axis_index("seg") * samples, chunk)
    at = 0
    for step, first, count in blocks:
        terms[pl.ds(at, count), :] = inner_ref[pl.ds(step * actuators + first, count), :]
        at += count
    terms[...] += jnp.dot(masked[...], sensed_ref[...], preferred_element_type=jnp.float32)


def outer_first_kernel(
    steps, samples, turned_in_ref, runs_ref, offsets_ref, mine_ref, theirs_ref, sensed_ref, inner_ref,
    turned, send_ref, *scratch
):
    far = lax.axis_size("seg") // 2
    half = turned.shape[0] // 2
    terms = scratch[3]
    blocks = [(step, 0, half) for step in steps]
    outer_terms(
        blocks, samples, runs_ref, offsets_ref, turned, sensed_ref, inner_ref, *scratch, tails=(mine_ref, theirs_ref)
    )
    rows = half // far
    size = rows * (terms.shape[1] // LANES)
    codes = []
    for number in range(len(steps)):
        parts = [terms[pl.ds(number * half + block * rows, rows), :] for block in range(far)]
        codes.append(put(send_ref, number * far * size, parts, size))
    put_codes(send_ref, len(steps) * far * size, codes)


def outer_rest_kernel(
    steps, samples, runs_ref, offsets_ref, turned, sensed_ref, inner_ref,
    own_group_ref, send_one_ref, send_own_ref, kept_one_ref, own_ref, *scratch
):
    far = lax.axis_size("seg") // 2
    actuators = turned.shape[0]
    half = actuators // 2
    terms = scratch[3]
    blocks = [(1, 0, actuators), (0, 0, actuators)] + [(step, half, half) for step in steps]
    outer_terms(blocks, samples, runs_ref, offsets_ref, turned, sensed_ref, inner_ref, *scratch)
    rows = half // far
    size = rows * (terms.shape[1] // LANES)

    def send(ref, at):
        parts = [terms[pl.ds(at + block * rows, rows), :] for block in range(far)]
        put_codes(ref, far * size, [put(ref, 0, parts, size)])

    send(send_one_ref, 0)
    send(send_own_ref, actuators)
    send(kept_one_ref, half)
    own_ref[...] = terms[pl.ds(actuators + half, half), :]
    own_group_ref[...] = terms[pl.ds(2 * actuators, len(steps) * half), :]


def second_near_kernel(came_one_ref, came_own_ref, kept_one_ref, own_ref, total_ref, *far_refs):
    far = lax.axis_size("seg") // 2
    far_refs = (None,) + far_refs
    rows, sensors = total_ref.shape[0] // 2, total_ref.shape[1]
    size = rows * (sensors // LANES)
    far_at = lax.axis_index("seg") // 2
    one, own, kept = (
        scales_of(ref, far * size, 1, sensors) for ref in (came_one_ref, came_own_ref, kept_one_ref)
    )

    def block_sum(step, block):
        at = pl.multiple_of(block * size, rows)
        if step:
            return opened(came_one_ref, at, one, 0, rows, sensors) + opened(kept_one_ref, at, kept, 0, rows, sensors)
        mine = own_ref[pl.ds(pl.multiple_of(block * rows, rows), rows), :]
        return mine + opened(came_own_ref, at, own, 0, rows, sensors)

    for bits in range(far - 1, 0, -1):
        codes = [put(far_refs[bits], step * size, [block_sum(step, far_at ^ bits)], size) for step in range(2)]
        put_codes(far_refs[bits], 2 * size, codes)
    for step in range(2):
        total_ref[pl.ds(step * rows, rows), :] = block_sum(step, far_at)


def far_sum(start, came, scales, number, rows, sensors):
    value = start
    size = rows * (sensors // LANES)
    for ref, scale in zip(came, scales):
        value = value + opened(ref, pl.multiple_of(number * size, rows), scale, number, rows, sensors)
    return value


def second_kernel(count, came_ref, own_ref, total_ref, *far_refs):
    far = lax.axis_size("seg") // 2
    far_refs = (None,) + far_refs
    rows, sensors = total_ref.shape[0] // count, total_ref.shape[1]
    size = rows * (sensors // LANES)
    far_at = lax.axis_index("seg") // 2
    scales = scales_of(came_ref, count * far * size, count, sensors)

    def block_sum(number, block):
        at = number * far + block
        return own_ref[pl.ds(pl.multiple_of(at * rows, rows), rows), :] + opened(
            came_ref, pl.multiple_of(at * size, rows), scales, number, rows, sensors
        )

    for bits in range(far - 1, 0, -1):
        codes = [put(far_refs[bits], number * size, [block_sum(number, far_at ^ bits)], size) for number in range(count)]
        put_codes(far_refs[bits], count * size, codes)
    for number in range(count):
        total_ref[pl.ds(number * rows, rows), :] = block_sum(number, far_at)


def third_kernel(count, total_ref, *refs):
    came, outs = refs[:-count], refs[-count:]
    rows, sensors = total_ref.shape[0] // count, total_ref.shape[1]
    size = rows * (sensors // LANES)
    scales = [scales_of(ref, count * size, count, sensors) for ref in came]
    for number in range(count):
        value = far_sum(total_ref[pl.ds(number * rows, rows), :], came, scales, number, rows, sensors)
        put_codes(outs[number], size, [put(outs[number], 0, [value], size)])


def last_kernel(scaling, steps, total_ref, *refs):
    far = lax.axis_size("seg") // 2
    out_ref, ready, sems = refs[-3:]
    came_far, came = refs[: far - 1], refs[far - 1 : -3]
    rows, sensors = total_ref.shape[0] // 2, total_ref.shape[1]
    size = rows * (sensors // LANES)
    lag = lax.axis_index("lag")
    copies = []

    def write(step, value):
        there = pl.ds(pl.multiple_of((lag ^ step) * sensors, LANES), sensors)
        ready[:, 0, there] = value * scaling
        copies.append(pltpu.make_async_copy(ready.at[:, :, there], out_ref.at[:, :, there], sems.at[step]))
        copies[-1].start()

    for number, step in enumerate(steps):
        write(step, opened(came[number], 0, scales_of(came[number], size, 1, sensors), 0, rows, sensors))
    scales = [scales_of(ref, 2 * size, 2, sensors) for ref in came_far]
    for step in range(2):
        write(step, far_sum(total_ref[pl.ds(step * rows, rows), :], came_far, scales, step, rows, sensors))
    for copy in copies:
        copy.wait()


def per_device_staged(actuator_input, sensor_output, run_lengths, lag_offsets):
    samples, actuators = actuator_input.shape
    sensors = sensor_output.shape[1]
    segs, lags = lax.axis_size("seg"), lax.axis_size("lag")
    far, rows, chunk = segs // 2, actuators // segs, LMAX
    scaling = 1.0 / math.sqrt(samples * segs)
    spare = lags * actuators

    def payload(count, codes):
        return jax.ShapeDtypeStruct(
            (count * rows * (sensors // LANES) + scale_rows(codes, sensors), LANES), jnp.int16
        )

    def wide(count):
        return jax.ShapeDtypeStruct((count * rows, sensors), jnp.float32)

    vmem = pl.BlockSpec(memory_space=pltpu.VMEM)
    small = pltpu.CompilerParams(vmem_limit_bytes=8 << 20)
    hbm = pl.BlockSpec(memory_space=pltpu.HBM)
    scalars = [pltpu.SMEM(run_lengths.shape, jnp.int32), pltpu.SMEM(lag_offsets.shape, jnp.int32)]
    chunks = samples // chunk
    run_lengths, lag_offsets, actuator_input, sensor_output = (
        pltpu.with_memory_space_constraint(value, pltpu.HBM)
        for value in (run_lengths, lag_offsets, actuator_input, sensor_output)
    )

    cut = pl.pallas_call(
        cut_kernel,
        in_specs=[hbm],
        out_specs=vmem,
        out_shape=jax.ShapeDtypeStruct((LMAX // 2, actuators), jnp.bfloat16),
        scratch_shapes=[pltpu.SemaphoreType.DMA],
        compiler_params=small,
        name="cut",
    )(actuator_input)
    fetched = shifted_by(cut, "seg", 1)
    swapped = exchange(fetched, 0, 1)

    across = jax.ShapeDtypeStruct((actuators, 2 * chunk + LANES), jnp.bfloat16)
    inner, first_turned, first_sensed, runs_held, offsets_held = pl.pallas_call(
        inner_kernel,
        in_specs=[hbm] * 4,
        out_specs=[vmem] * 5,
        out_shape=[
            jax.ShapeDtypeStruct((spare, sensors), jnp.float32),
            across,
            jax.ShapeDtypeStruct((chunk, sensors), jnp.bfloat16),
            jax.ShapeDtypeStruct(run_lengths.shape, jnp.int32),
            jax.ShapeDtypeStruct(lag_offsets.shape, jnp.int32),
        ],
        scratch_shapes=scalars
        + [
            pltpu.VMEM((samples, actuators), jnp.bfloat16),
            pltpu.VMEM((samples - chunk, sensors), jnp.bfloat16),
            pltpu.VMEM((actuators, samples + LANES), jnp.bfloat16),
            pltpu.VMEM((spare, samples - chunk), jnp.bfloat16),
            pltpu.SemaphoreType.DMA((4 + 2 * chunks,)),
        ],
        compiler_params=pltpu.CompilerParams(vmem_limit_bytes=40 << 20),
        cost_estimate=pl.CostEstimate(
            flops=2 * spare * sensors * (samples - chunk), bytes_accessed=6 << 20, transcendentals=0
        ),
        name="inner",
    )(run_lengths, lag_offsets, actuator_input, sensor_output)

    def outer(name, body, count, shapes, aliases, *operands):
        return pl.pallas_call(
            body,
            in_specs=[vmem] * len(operands),
            out_specs=[vmem] * len(shapes),
            out_shape=shapes,
            input_output_aliases=aliases,
            scratch_shapes=scalars
            + [
                pltpu.VMEM((count, chunk), jnp.bfloat16),
                pltpu.VMEM((count, sensors), jnp.float32),
                pltpu.SemaphoreType.DMA((2,)),
            ],
            compiler_params=pltpu.CompilerParams(vmem_limit_bytes=24 << 20),
            cost_estimate=pl.CostEstimate(
                flops=2 * count * sensors * chunk, bytes_accessed=4 << 20, transcendentals=0
            ),
            name=name,
        )(*operands)

    def local(name, body, shapes, *operands):
        return pl.pallas_call(
            body,
            in_specs=[vmem] * len(operands),
            out_specs=[vmem] * len(shapes),
            out_shape=shapes,
            compiler_params=small,
            cost_estimate=pl.CostEstimate(flops=1 << 20, bytes_accessed=1 << 20, transcendentals=0),
            name=name,
        )(*operands)

    def far_exchange(sends):
        came = [None] * (far - 1)
        for bits in range(far - 1, 0, -1):
            came[bits - 1] = exchange(sends[bits - 1], 2 * bits, 0)
        return came

    steps = tuple(range(lags - 1, 1, -1))
    count = len(steps)

    def outer_a(*refs):
        outer_first_kernel(steps, samples, *refs)

    def outer_b(*refs):
        outer_rest_kernel(steps, samples, *refs)

    def second_a(*refs):
        second_kernel(count, *refs)

    def third_a(*refs):
        third_kernel(count, *refs)

    def last_body(*refs):
        last_kernel(scaling, steps, *refs)

    turned, send_a = outer(
        "outer_a",
        outer_a,
        count * actuators // 2,
        [across, payload(count * far, count)],
        {0: 0},
        first_turned,
        runs_held,
        offsets_held,
        fetched,
        swapped,
        first_sensed,
        inner,
    )
    came_a = exchange(send_a, 1, 0)
    own_a, send_one, send_own, kept_one, own_b = outer(
        "outer_b",
        outer_b,
        (4 + count) * actuators // 2,
        [wide(count * far)] + [payload(far, 1)] * 3 + [wide(far)],
        {},
        runs_held,
        offsets_held,
        turned,
        first_sensed,
        inner,
    )
    came_one = exchange(send_one, 1, 1)
    came_own = exchange(send_own, 1, 0)
    kept_one = exchange(kept_one, 0, 1)
    total_a, *sends_a = local("second_a", second_a, [wide(count)] + [payload(count, count)] * (far - 1), came_a, own_a)
    far_a = far_exchange(sends_a)
    total_b, *sends_b = local(
        "second_b",
        second_near_kernel,
        [wide(2)] + [payload(2, 2)] * (far - 1),
        came_one,
        came_own,
        kept_one,
        own_b,
    )
    far_b = far_exchange(sends_b)
    outs = local("third_a", third_a, [payload(1, 1)] * count, total_a, *far_a)
    came = [exchange(out, 0, step) for step, out in zip(steps, outs)]
    return pl.pallas_call(
        last_body,
        in_specs=[vmem] * (far + count),
        out_specs=hbm,
        out_shape=jax.ShapeDtypeStruct((rows, 1, lags * sensors), jnp.float32),
        scratch_shapes=[
            pltpu.VMEM((rows, 1, lags * sensors), jnp.float32),
            pltpu.SemaphoreType.DMA((lags,)),
        ],
        compiler_params=small,
        name="last",
    )(total_b, *far_b, *came)


def solution(mesh):
    segs, lags = mesh.shape["seg"], mesh.shape["lag"]

    def per_device(actuator_input, sensor_output, run_lengths, lag_offsets):
        rows, sensors = actuator_input.shape[1] // segs, sensor_output.shape[1]
        staged = (
            4 <= segs <= 16
            and segs & (segs - 1) == 0
            and lags & (lags - 1) == 0
            and lags == NBLK * LBW
            and lags >= 4
            and rows % 8 == 0
            and sensors % LANES == 0
            and actuator_input.shape[0] % LMAX == 0
            and actuator_input.shape[0] > LMAX
        )
        chosen = per_device_staged if staged else per_device_plain
        return chosen(actuator_input, sensor_output, run_lengths, lag_offsets)

    return jax.shard_map(
        per_device,
        mesh=mesh,
        in_specs=(P("seg", None), P("seg", "lag"), P(), P()),
        out_specs=P("seg", "lag", None),
        check_vma=False,
    )
```

```python
import math

import jax
import jax.numpy as jnp
from jax import lax
from jax.experimental import pallas as pl
from jax.experimental.pallas import tpu as pltpu
from jax.experimental import pallas as pl
from jax.experimental.pallas import tpu as pltpu
from jax.experimental import pallas as pl
from jax.experimental.pallas import tpu as pltpu
from jax.experimental import pallas as pl
from jax.experimental.pallas import tpu as pltpu
from jax.experimental import pallas as pl
from jax.experimental.pallas import tpu as pltpu
from jax.experimental import pallas as pl
from jax.experimental.pallas import tpu as pltpu
from jax.experimental import pallas as pl
from jax.experimental.pallas import tpu as pltpu
from jax.sharding import PartitionSpec as P


LMAX = 1024
LBW = 2
NBLK = 2
FINE = 64.0
FULL = 32700.0
LEAST = -112.0 * FINE
SCALE_ROWS = 8
LANES = 128
LANES = 128
LANES = 128
LANES = 128
LANES = 128
LANES = 128
LANES = 128


def shifted_by(value, axis, steps):
    count = lax.axis_size(axis)
    initial, last = (max(0, -steps), min(count, count - steps))
    return lax.ppermute(value, axis, [(source, source + steps) for source in range(initial, last)])


def segment_ids(run_lengths, start_row, row_count):
    run_ends = jnp.cumsum(run_lengths)
    places = start_row + jnp.arange(row_count, dtype=jnp.int32)
    return jnp.sum((run_ends[None, :] <= places[:, None]).astype(jnp.int32), axis=1)


def product_over_time(masked, shifted):
    return lax.dot_general(
        masked, shifted, (((0,), (0,)), ((), ())), preferred_element_type=jnp.float32
    )


def per_device_plain(actuator_input, sensor_output, run_lengths, lag_offsets):
    samples = actuator_input.shape[0]
    devices_seg = lax.axis_size("seg")
    scaling = 1.0 / math.sqrt(samples * devices_seg)
    start_row = lax.axis_index("seg") * samples
    halo_rows = shifted_by(sensor_output[:LMAX], "seg", -1)
    idents = segment_ids(run_lengths, start_row, samples + LMAX)
    own_ids = idents[:samples]
    shifts = [lag_offsets[blk_num] + lag_step for blk_num in range(NBLK) for lag_step in range(LBW)]
    joined = jnp.concatenate([sensor_output, halo_rows], axis=0)

    def lag_term(lag_value):
        shifted = lax.dynamic_slice_in_dim(joined, lag_value, samples, 0)
        shifted_ids = lax.dynamic_slice_in_dim(idents, lag_value, samples, 0)
        masked = jnp.where((own_ids == shifted_ids)[:, None], actuator_input, jnp.zeros_like(actuator_input))
        return product_over_time(masked, shifted)

    shares = lax.psum_scatter(
        jnp.stack([lag_term(lag_value) for lag_value in shifts], axis=1),
        "seg",
        scatter_dimension=0,
        tiled=True,
    )
    result_rows = lax.all_to_all(shares, "lag", split_axis=1, concat_axis=2, tiled=True)
    return result_rows * scaling


def exchange(value, seg_bits, lag_bits):
    segs, lags = lax.axis_size("seg"), lax.axis_size("lag")
    pairs = [
        (s * lags + l, (s ^ seg_bits) * lags + (l ^ lag_bits)) for s in range(segs) for l in range(lags)
    ]
    return lax.ppermute(value, ("seg", "lag"), pairs)


def column_code(largest):
    return jnp.maximum(jnp.ceil(jnp.log2(largest) * FINE), LEAST)


def scale_rows(count, width):
    return -(-count * (width // LANES) // SCALE_ROWS) * SCALE_ROWS


def put(ref, at, parts, stride):
    largest = jnp.abs(parts[0])
    for part in parts[1:]:
        largest = jnp.maximum(largest, jnp.abs(part))
    code = column_code(jnp.max(largest, axis=0, keepdims=True))
    factor = jnp.exp2(code * (-1.0 / FINE)) * FULL
    rows, width = parts[0].shape
    for number, part in enumerate(parts):
        held = jnp.round(part * factor).astype(jnp.int32).astype(jnp.int16)
        for lanes in range(width // LANES):
            ref[pl.ds(at + number * stride + lanes * rows, rows), :] = held[:, lanes * LANES : (lanes + 1) * LANES]
    return code


def put_codes(ref, at, codes):
    width = codes[0].shape[1]
    pieces = [code[:, start : start + LANES] for code in codes for start in range(0, width, LANES)]
    count = scale_rows(len(codes), width)
    shape = (count, LANES)
    sublane = lax.broadcasted_iota(jnp.int32, shape, 0)
    rows = jnp.broadcast_to(pieces[0].astype(jnp.int32), shape)
    for row in range(1, len(pieces)):
        rows = jnp.where(sublane == row, jnp.broadcast_to(pieces[row].astype(jnp.int32), shape), rows)
    ref[pl.ds(at, count), :] = rows.astype(jnp.int16)


def scales_of(ref, at, count, width):
    codes = ref[pl.ds(at, scale_rows(count, width)), :].astype(jnp.int32).astype(jnp.float32)
    return jnp.exp2(codes * (1.0 / FINE)) * (1.0 / FULL)


def opened(ref, at, scales, number, rows, width):
    lanes = width // LANES
    return jnp.concatenate(
        [
            ref[pl.ds(at + block * rows, rows), :].astype(jnp.float32)
            * scales[number * lanes + block : number * lanes + block + 1]
            for block in range(lanes)
        ],
        axis=1,
    )


def lag_of(offsets_ref, which):
    return offsets_ref[which // LBW] + which % LBW


def put_turned(turned, at_lane, value):
    segs = lax.axis_size("seg")
    actuators = value.shape[1]
    rows, near_at = actuators // segs, lax.axis_index("seg") % 2
    across = value.T
    for at in range(segs):
        mine = (near_at + at + 1) % 2
        start = mine * (actuators // 2) + (at // 2) * rows
        turned[pl.ds(pl.multiple_of(start, rows), rows), pl.ds(at_lane, value.shape[0])] = across[
            at * rows : (at + 1) * rows
        ]


def fill_rows(turned, at_lane, masked, at_masked, runs, offsets, lag, blocks, start_row, chunk):
    tiles = chunk // LANES
    lane = lax.broadcasted_iota(jnp.int32, (1, LANES), 1)
    ends, end = [], jnp.int32(0)
    for run in range(runs.shape[0]):
        end = end + runs[run]
        ends.append(end)
    at_row = 0
    for step, first_row, actuators in blocks:
        shift = lag_of(offsets, lag ^ step)
        at = at_lane - shift
        base, turn = at // LANES, at % LANES
        low = jnp.broadcast_to(lane < LANES - turn, (actuators, LANES))
        pieces = [
            pltpu.roll(
                turned[
                    pl.ds(first_row, actuators), pl.ds(pl.multiple_of((base + tile) * LANES, LANES), LANES)
                ],
                (LANES - turn) % LANES,
                1,
            )
            for tile in range(tiles + 1)
        ]
        for tile in range(tiles):
            place = lane + (start_row + tile * LANES)
            crossed = jnp.zeros((1, LANES), jnp.int32)
            for end in ends:
                crossed = crossed + ((end <= place) & (end > place - shift)).astype(jnp.int32)
            keep = jnp.broadcast_to(crossed == 0, (actuators, LANES))
            value = jnp.where(low, pieces[tile], pieces[tile + 1])
            value = jnp.where(keep, value, jnp.zeros_like(value))
            masked[pl.ds(at_row, actuators), pl.ds(at_masked + tile * LANES, LANES)] = value
        at_row += actuators


def inner_kernel(
    runs_ref, offsets_ref, actuators_ref, sensors_ref, out_ref, first_turned_ref, first_sensed_ref,
    runs_out, offsets_out, runs, offsets, held, sensed, turned, masked, sems
):
    chunk, lags = LMAX, lax.axis_size("lag")
    samples, actuators = actuators_ref.shape
    chunks = samples // chunk
    copies = [
        pltpu.make_async_copy(runs_ref, runs, sems.at[0]),
        pltpu.make_async_copy(offsets_ref, offsets, sems.at[1]),
    ]
    for at in range(chunks):
        here = pl.ds(at * chunk, chunk)
        copies.append(pltpu.make_async_copy(actuators_ref.at[here, :], held.at[here, :], sems.at[2 + at]))
    for at in range(1, chunks):
        copies.append(
            pltpu.make_async_copy(
                sensors_ref.at[pl.ds(at * chunk, chunk), :],
                sensed.at[pl.ds((at - 1) * chunk, chunk), :],
                sems.at[1 + chunks + at],
            )
        )
    copies.append(
        pltpu.make_async_copy(sensors_ref.at[pl.ds(0, chunk), :], first_sensed_ref, sems.at[1 + 2 * chunks])
    )
    copies.append(pltpu.make_async_copy(runs_ref, runs_out, sems.at[2 + 2 * chunks]))
    copies.append(pltpu.make_async_copy(offsets_ref, offsets_out, sems.at[3 + 2 * chunks]))
    for copy in copies:
        copy.start()
    start_row = lax.axis_index("seg") * samples
    for at in range(chunks):
        copies[2 + at].wait()
        here = pl.ds(at * chunk, chunk)
        put_turned(turned, at * chunk, held[here, :])
        if at == 0:
            first_turned_ref[:, pl.ds(chunk, chunk)] = turned[:, here]
            copies[0].wait()
            copies[1].wait()
            continue
        fill_rows(
            turned, at * chunk, masked, (at - 1) * chunk, runs, offsets,
            lax.axis_index("lag"), [(step, 0, actuators) for step in range(lags)], start_row + at * chunk, chunk,
        )
        copies[1 + chunks + at].wait()
        there = pl.ds((at - 1) * chunk, chunk)
        terms = jnp.dot(masked[:, there], sensed[there, :], preferred_element_type=jnp.float32)
        if at == 1:
            out_ref[...] = terms
        else:
            out_ref[...] += terms
    for copy in copies[-3:]:
        copy.wait()


def cut_kernel(actuators_ref, out_ref, sem):
    half = out_ref.shape[0]
    start = actuators_ref.shape[0] - LMAX + half * (lax.axis_index("lag") % 2)
    copy = pltpu.make_async_copy(actuators_ref.at[pl.ds(pl.multiple_of(start, 8), half), :], out_ref, sem)
    copy.start()
    copy.wait()


def outer_terms(
    blocks, samples, runs_ref, offsets_ref, turned, sensed_ref, inner_ref, runs, offsets, masked, terms, sems, tails=()
):
    chunk = LMAX
    copies = [
        pltpu.make_async_copy(runs_ref, runs, sems.at[0]),
        pltpu.make_async_copy(offsets_ref, offsets, sems.at[1]),
    ]
    for copy in copies:
        copy.start()
    actuators = inner_ref.shape[0] // lax.axis_size("lag")
    lag, half = lax.axis_index("lag"), chunk // 2
    for number, tail_ref in enumerate(tails):
        place = (lag + number) % 2
        put_turned(turned, pl.multiple_of(place * half, LANES), tail_ref[...])
    for copy in copies:
        copy.wait()
    fill_rows(turned, chunk, masked, 0, runs, offsets, lag, blocks, lax.axis_index("seg") * samples, chunk)
    at = 0
    for step, first, count in blocks:
        terms[pl.ds(at, count), :] = inner_ref[pl.ds(step * actuators + first, count), :]
        at += count
    terms[...] += jnp.dot(masked[...], sensed_ref[...], preferred_element_type=jnp.float32)


def outer_first_kernel(
    steps, samples, turned_in_ref, runs_ref, offsets_ref, mine_ref, theirs_ref, sensed_ref, inner_ref,
    turned, send_ref, *scratch
):
    far = lax.axis_size("seg") // 2
    half = turned.shape[0] // 2
    terms = scratch[3]
    blocks = [(step, 0, half) for step in steps]
    outer_terms(
        blocks, samples, runs_ref, offsets_ref, turned, sensed_ref, inner_ref, *scratch, tails=(mine_ref, theirs_ref)
    )
    rows = half // far
    size = rows * (terms.shape[1] // LANES)
    codes = []
    for number in range(len(steps)):
        parts = [terms[pl.ds(number * half + block * rows, rows), :] for block in range(far)]
        codes.append(put(send_ref, number * far * size, parts, size))
    put_codes(send_ref, len(steps) * far * size, codes)


def outer_rest_kernel(
    steps, samples, runs_ref, offsets_ref, turned, sensed_ref, inner_ref,
    own_group_ref, send_one_ref, send_own_ref, kept_one_ref, own_ref, *scratch
):
    far = lax.axis_size("seg") // 2
    actuators = turned.shape[0]
    half = actuators // 2
    terms = scratch[3]
    blocks = [(1, 0, actuators), (0, 0, actuators)] + [(step, half, half) for step in steps]
    outer_terms(blocks, samples, runs_ref, offsets_ref, turned, sensed_ref, inner_ref, *scratch)
    rows = half // far
    size = rows * (terms.shape[1] // LANES)

    def send(ref, at):
        parts = [terms[pl.ds(at + block * rows, rows), :] for block in range(far)]
        put_codes(ref, far * size, [put(ref, 0, parts, size)])

    send(send_one_ref, 0)
    send(send_own_ref, actuators)
    send(kept_one_ref, half)
    own_ref[...] = terms[pl.ds(actuators + half, half), :]
    own_group_ref[...] = terms[pl.ds(2 * actuators, len(steps) * half), :]


def second_near_kernel(came_one_ref, came_own_ref, kept_one_ref, own_ref, total_ref, *far_refs):
    far = lax.axis_size("seg") // 2
    far_refs = (None,) + far_refs
    rows, sensors = total_ref.shape[0] // 2, total_ref.shape[1]
    size = rows * (sensors // LANES)
    far_at = lax.axis_index("seg") // 2
    one, own, kept = (
        scales_of(ref, far * size, 1, sensors) for ref in (came_one_ref, came_own_ref, kept_one_ref)
    )

    def block_sum(step, block):
        at = pl.multiple_of(block * size, rows)
        if step:
            return opened(came_one_ref, at, one, 0, rows, sensors) + opened(kept_one_ref, at, kept, 0, rows, sensors)
        mine = own_ref[pl.ds(pl.multiple_of(block * rows, rows), rows), :]
        return mine + opened(came_own_ref, at, own, 0, rows, sensors)

    for bits in range(far - 1, 0, -1):
        codes = [put(far_refs[bits], step * size, [block_sum(step, far_at ^ bits)], size) for step in range(2)]
        put_codes(far_refs[bits], 2 * size, codes)
    for step in range(2):
        total_ref[pl.ds(step * rows, rows), :] = block_sum(step, far_at)


def far_sum(start, came, scales, number, rows, sensors):
    value = start
    size = rows * (sensors // LANES)
    for ref, scale in zip(came, scales):
        value = value + opened(ref, pl.multiple_of(number * size, rows), scale, number, rows, sensors)
    return value


def second_kernel(count, came_ref, own_ref, total_ref, *far_refs):
    far = lax.axis_size("seg") // 2
    far_refs = (None,) + far_refs
    rows, sensors = total_ref.shape[0] // count, total_ref.shape[1]
    size = rows * (sensors // LANES)
    far_at = lax.axis_index("seg") // 2
    scales = scales_of(came_ref, count * far * size, count, sensors)

    def block_sum(number, block):
        at = number * far + block
        return own_ref[pl.ds(pl.multiple_of(at * rows, rows), rows), :] + opened(
            came_ref, pl.multiple_of(at * size, rows), scales, number, rows, sensors
        )

    for bits in range(far - 1, 0, -1):
        codes = [put(far_refs[bits], number * size, [block_sum(number, far_at ^ bits)], size) for number in range(count)]
        put_codes(far_refs[bits], count * size, codes)
    for number in range(count):
        total_ref[pl.ds(number * rows, rows), :] = block_sum(number, far_at)


def third_kernel(count, total_ref, *refs):
    came, outs = refs[:-count], refs[-count:]
    rows, sensors = total_ref.shape[0] // count, total_ref.shape[1]
    size = rows * (sensors // LANES)
    scales = [scales_of(ref, count * size, count, sensors) for ref in came]
    for number in range(count):
        value = far_sum(total_ref[pl.ds(number * rows, rows), :], came, scales, number, rows, sensors)
        put_codes(outs[number], size, [put(outs[number], 0, [value], size)])


def last_kernel(scaling, steps, total_ref, *refs):
    far = lax.axis_size("seg") // 2
    out_ref, ready, sems = refs[-3:]
    came_far, came = refs[: far - 1], refs[far - 1 : -3]
    rows, sensors = total_ref.shape[0] // 2, total_ref.shape[1]
    size = rows * (sensors // LANES)
    lag = lax.axis_index("lag")
    copies = []

    def write(step, value):
        there = pl.ds(pl.multiple_of((lag ^ step) * sensors, LANES), sensors)
        ready[:, 0, there] = value * scaling
        copies.append(pltpu.make_async_copy(ready.at[:, :, there], out_ref.at[:, :, there], sems.at[step]))
        copies[-1].start()

    for number, step in enumerate(steps):
        write(step, opened(came[number], 0, scales_of(came[number], size, 1, sensors), 0, rows, sensors))
    scales = [scales_of(ref, 2 * size, 2, sensors) for ref in came_far]
    for step in range(2):
        write(step, far_sum(total_ref[pl.ds(step * rows, rows), :], came_far, scales, step, rows, sensors))
    for copy in copies:
        copy.wait()


def per_device_staged(actuator_input, sensor_output, run_lengths, lag_offsets):
    samples, actuators = actuator_input.shape
    sensors = sensor_output.shape[1]
    segs, lags = lax.axis_size("seg"), lax.axis_size("lag")
    far, rows, chunk = segs // 2, actuators // segs, LMAX
    scaling = 1.0 / math.sqrt(samples * segs)
    spare = lags * actuators

    def payload(count, codes):
        return jax.ShapeDtypeStruct(
            (count * rows * (sensors // LANES) + scale_rows(codes, sensors), LANES), jnp.int16
        )

    def wide(count):
        return jax.ShapeDtypeStruct((count * rows, sensors), jnp.float32)

    vmem = pl.BlockSpec(memory_space=pltpu.VMEM)
    small = pltpu.CompilerParams(vmem_limit_bytes=8 << 20)
    hbm = pl.BlockSpec(memory_space=pltpu.HBM)
    scalars = [pltpu.SMEM(run_lengths.shape, jnp.int32), pltpu.SMEM(lag_offsets.shape, jnp.int32)]
    chunks = samples // chunk
    run_lengths, lag_offsets, actuator_input, sensor_output = (
        pltpu.with_memory_space_constraint(value, pltpu.HBM)
        for value in (run_lengths, lag_offsets, actuator_input, sensor_output)
    )

    cut = pl.pallas_call(
        cut_kernel,
        in_specs=[hbm],
        out_specs=vmem,
        out_shape=jax.ShapeDtypeStruct((LMAX // 2, actuators), jnp.bfloat16),
        scratch_shapes=[pltpu.SemaphoreType.DMA],
        compiler_params=small,
        name="cut",
    )(actuator_input)
    fetched = shifted_by(cut, "seg", 1)
    swapped = exchange(fetched, 0, 1)

    across = jax.ShapeDtypeStruct((actuators, 2 * chunk + LANES), jnp.bfloat16)
    inner, first_turned, first_sensed, runs_held, offsets_held = pl.pallas_call(
        inner_kernel,
        in_specs=[hbm] * 4,
        out_specs=[vmem] * 5,
        out_shape=[
            jax.ShapeDtypeStruct((spare, sensors), jnp.float32),
            across,
            jax.ShapeDtypeStruct((chunk, sensors), jnp.bfloat16),
            jax.ShapeDtypeStruct(run_lengths.shape, jnp.int32),
            jax.ShapeDtypeStruct(lag_offsets.shape, jnp.int32),
        ],
        scratch_shapes=scalars
        + [
            pltpu.VMEM((samples, actuators), jnp.bfloat16),
            pltpu.VMEM((samples - chunk, sensors), jnp.bfloat16),
            pltpu.VMEM((actuators, samples + LANES), jnp.bfloat16),
            pltpu.VMEM((spare, samples - chunk), jnp.bfloat16),
            pltpu.SemaphoreType.DMA((4 + 2 * chunks,)),
        ],
        compiler_params=pltpu.CompilerParams(vmem_limit_bytes=40 << 20),
        cost_estimate=pl.CostEstimate(
            flops=2 * spare * sensors * (samples - chunk), bytes_accessed=6 << 20, transcendentals=0
        ),
        name="inner",
    )(run_lengths, lag_offsets, actuator_input, sensor_output)

    def outer(name, body, count, shapes, aliases, *operands):
        return pl.pallas_call(
            body,
            in_specs=[vmem] * len(operands),
            out_specs=[vmem] * len(shapes),
            out_shape=shapes,
            input_output_aliases=aliases,
            scratch_shapes=scalars
            + [
                pltpu.VMEM((count, chunk), jnp.bfloat16),
                pltpu.VMEM((count, sensors), jnp.float32),
                pltpu.SemaphoreType.DMA((2,)),
            ],
            compiler_params=pltpu.CompilerParams(vmem_limit_bytes=24 << 20),
            cost_estimate=pl.CostEstimate(
                flops=2 * count * sensors * chunk, bytes_accessed=4 << 20, transcendentals=0
            ),
            name=name,
        )(*operands)

    def local(name, body, shapes, *operands):
        return pl.pallas_call(
            body,
            in_specs=[vmem] * len(operands),
            out_specs=[vmem] * len(shapes),
            out_shape=shapes,
            compiler_params=small,
            cost_estimate=pl.CostEstimate(flops=1 << 20, bytes_accessed=1 << 20, transcendentals=0),
            name=name,
        )(*operands)

    def far_exchange(sends, masks):
        came = [None] * (far - 1)
        for bits in masks:
            came[bits - 1] = exchange(sends[bits - 1], 2 * bits, 0)
        return came

    steps = tuple(range(lags - 1, 1, -1))
    count = len(steps)

    def outer_a(*refs):
        outer_first_kernel(steps, samples, *refs)

    def outer_b(*refs):
        outer_rest_kernel(steps, samples, *refs)

    def second_a(*refs):
        second_kernel(count, *refs)

    def third_a(*refs):
        third_kernel(count, *refs)

    def last_body(*refs):
        last_kernel(scaling, steps, *refs)

    turned, send_a = outer(
        "outer_a",
        outer_a,
        count * actuators // 2,
        [across, payload(count * far, count)],
        {0: 0},
        first_turned,
        runs_held,
        offsets_held,
        fetched,
        swapped,
        first_sensed,
        inner,
    )
    came_a = exchange(send_a, 1, 0)
    own_a, send_one, send_own, kept_one, own_b = outer(
        "outer_b",
        outer_b,
        (4 + count) * actuators // 2,
        [wide(count * far)] + [payload(far, 1)] * 3 + [wide(far)],
        {},
        runs_held,
        offsets_held,
        turned,
        first_sensed,
        inner,
    )
    came_one = exchange(send_one, 1, 1)
    came_own = exchange(send_own, 1, 0)
    kept_one = exchange(kept_one, 0, 1)
    total_a, *sends_a = local("second_a", second_a, [wide(count)] + [payload(count, count)] * (far - 1), came_a, own_a)
    far_a = far_exchange(sends_a, (2, 3, 1))
    total_b, *sends_b = local(
        "second_b",
        second_near_kernel,
        [wide(2)] + [payload(2, 2)] * (far - 1),
        came_one,
        came_own,
        kept_one,
        own_b,
    )
    far_b = far_exchange(sends_b, (3, 1, 2))
    outs = local("third_a", third_a, [payload(1, 1)] * count, total_a, *far_a)
    came = [exchange(out, 0, step) for step, out in zip(steps, outs)]
    return pl.pallas_call(
        last_body,
        in_specs=[vmem] * (far + count),
        out_specs=hbm,
        out_shape=jax.ShapeDtypeStruct((rows, 1, lags * sensors), jnp.float32),
        scratch_shapes=[
            pltpu.VMEM((rows, 1, lags * sensors), jnp.float32),
            pltpu.SemaphoreType.DMA((lags,)),
        ],
        compiler_params=small,
        name="last",
    )(total_b, *far_b, *came)


def solution(mesh):
    segs, lags = mesh.shape["seg"], mesh.shape["lag"]

    def per_device(actuator_input, sensor_output, run_lengths, lag_offsets):
        rows, sensors = actuator_input.shape[1] // segs, sensor_output.shape[1]
        staged = (
            4 <= segs <= 16
            and segs & (segs - 1) == 0
            and lags & (lags - 1) == 0
            and lags == NBLK * LBW
            and lags >= 4
            and rows % 8 == 0
            and sensors % LANES == 0
            and actuator_input.shape[0] % LMAX == 0
            and actuator_input.shape[0] > LMAX
        )
        chosen = per_device_staged if staged else per_device_plain
        return chosen(actuator_input, sensor_output, run_lengths, lag_offsets)

    return jax.shard_map(
        per_device,
        mesh=mesh,
        in_specs=(P("seg", None), P("seg", "lag"), P(), P()),
        out_specs=P("seg", "lag", None),
        check_vma=False,
    )
```
